128 devices in a mesh: rows: 64 (over z, y, x_hi, core), blk: 2 (over x_lo).
Axes of the slice: x: 4 (x_hi: 2, x_lo: 2; x = x_hi * 2 + x_lo), y: 4, z: 4, core: 2. Of those that a mesh axis runs over, the one named last changes fastest.
Arguments:
- text_emb: bfloat16 [16384, 4096], P('rows'), may hold values from -6 to 6
- quant_emb: bfloat16 [16384, 4096], P('rows'), may hold values from -6 to 6
- text_head: bfloat16 [4096, 2048], P(None, 'blk'), may hold values from -0.09375 to 0.09375
- quant_head: bfloat16 [4096, 2048], P(None, 'blk'), may hold values from -0.09375 to 0.09375
Outputs:
- grad_text: float32 [16384, 2048], P(('rows', 'blk'))
- grad_quant: float32 [16384, 2048], P(('rows', 'blk'))
The draws below stay inside these ranges and needn't reach their ends.
All inputs are finite; a program needn't handle non-finite values.
Results may differ from the reference program's by a relative error of at most 0.0049.
Values may be sent and summed in bfloat16 or wider, within the bound.
A program may use at most 256 MiB of HBM per device.

```python
import jax
import jax.numpy as jnp

EMB = 4096
D = 2048
TOTAL = 16384


def levels(own_key, extent, split, low, top_value):
    factor_of = 1.0
    for axis_at, shards_of in split:
        heights = jax.random.uniform(jax.random.fold_in(jax.random.fold_in(own_key, 6), axis_at), (shards_of,), jnp.float32, low / len(split), top_value / len(split))
        factor_of = factor_of * jnp.repeat(jnp.exp(heights), extent[axis_at] // shards_of).reshape((-1,) + (1,) * (len(extent) - 1 - axis_at))
    return factor_of


def normal_values(key, shape, spread, limit, split=(), held_as=jnp.bfloat16):
    factor_of = levels(key, shape, split, -0.22, 0.18) if split else 1.0
    result = jax.random.normal(key, shape, jnp.float32) * spread * factor_of
    return jnp.minimum(jnp.maximum(result, -limit), limit).astype(held_as)


def setup_inputs(seed: int = 0) -> dict:
    seeds = jax.random.split(jax.random.key(seed), 5)
    return {
        "text_emb": normal_values(seeds[0], (TOTAL, EMB), 1.0, 6.0, ((0, 64),)),
        "quant_emb": normal_values(seeds[1], (TOTAL, EMB), 1.0, 6.0, ((0, 64),)),
        "text_head": normal_values(seeds[2], (EMB, D), EMB ** -0.5, 0.09375, ((1, 2),)),
        "quant_head": normal_values(seeds[3], (EMB, D), EMB ** -0.5, 0.09375, ((1, 2),)),
    }


ridge_weight = 0.05

def whiten_pair(feat_one, feat_two):
    cov_one = jnp.dot(feat_one.T.astype(jnp.float32), feat_one.astype(jnp.float32), preferred_element_type=jnp.float32) / TOTAL
    cov_two = jnp.dot(feat_two.T.astype(jnp.float32), feat_two.astype(jnp.float32), preferred_element_type=jnp.float32) / TOTAL
    ident = jnp.eye(D, dtype=jnp.float32)
    factor_one = jnp.linalg.cholesky(cov_one + ridge_weight * ident)
    factor_two = jnp.linalg.cholesky(cov_two + ridge_weight * ident)
    white_one = jax.scipy.linalg.solve_triangular(factor_one, feat_one.astype(jnp.float32).T, lower=True)
    white_two = jax.scipy.linalg.solve_triangular(factor_two, feat_two.astype(jnp.float32).T, lower=True)
    grad_one = jax.scipy.linalg.solve_triangular(factor_one, white_two, lower=True, trans='T').T
    grad_two = jax.scipy.linalg.solve_triangular(factor_two, white_one, lower=True, trans='T').T
    return (grad_one, grad_two)

def reference(text_emb, quant_emb, text_head, quant_head):
    feat_text = jnp.dot(text_emb.astype(jnp.float32), text_head.astype(jnp.float32), preferred_element_type=jnp.float32).astype(jnp.bfloat16)
    feat_quant = jnp.dot(quant_emb.astype(jnp.float32), quant_head.astype(jnp.float32), preferred_element_type=jnp.float32).astype(jnp.bfloat16)
    grad_text, grad_quant = whiten_pair(feat_text, feat_quant)
    return (grad_text, grad_quant)
```

```python
import functools

import jax
import jax.numpy as jnp
from jax import lax
from jax.experimental import pallas as pl
from jax.experimental.pallas import tpu as pltpu
from jax.sharding import PartitionSpec as P

ridge_weight = 0.05
B = 256
NN = (((1,), (0,)), ((), ()))
NT = (((1,), (1,)), ((), ()))
TN = (((0,), (0,)), ((), ()))
MESH = pl.DeviceIdType.MESH
VMEM = pl.BlockSpec(memory_space=pltpu.VMEM)
HBM = pl.BlockSpec(memory_space=pl.ANY)


def mm(a, b, dims):
    return lax.dot_general(a, b, dims, preferred_element_type=jnp.float32)


def halves(x):
    hi = x.astype(jnp.bfloat16)
    return hi, (x - hi.astype(jnp.float32)).astype(jnp.bfloat16)


def dot3(a, b, dims):
    (ah, al), (bh, bl) = a, b
    return mm(ah, bh, dims) + (mm(ah, bl, dims) + mm(al, bh, dims))


def push(src, dst, send, recv, **device):
    return pltpu.make_async_remote_copy(
        src_ref=src, dst_ref=dst, send_sem=send, recv_sem=recv, device_id=device, device_id_type=MESH
    )


def covariance_kernel(
    peers, total, h_ref, feat_ref, cov_ref, feat, part, arrived, mine, x_send, x_recv, s_send, s_recv, g_send, g_recv, f_send, f_recv
):
    at = lax.axis_index("rows")
    view = lax.axis_index("blk")
    core, spot = lax.rem(at, 2), at // 2
    twin = at + 1 - 2 * core
    half_cols = h_ref.shape[2]
    chunk = mine.shape[0]
    blocks = part.shape[0] // B

    barrier = pltpu.get_barrier_semaphore()

    def greet(d, _):
        pl.semaphore_signal(
            barrier, inc=1, device_id={"rows": 2 * lax.rem(spot + d, peers) + core}, device_id_type=MESH
        )
        return 0

    lax.fori_loop(1, peers, greet, 0)
    pl.semaphore_signal(barrier, inc=1, device_id={"rows": twin}, device_id_type=MESH)
    pl.semaphore_signal(barrier, inc=1, device_id={"blk": 1 - view}, device_id_type=MESH)
    pl.semaphore_wait(barrier, peers + 1)

    swap = push(h_ref.at[1 - view], feat.at[core, view], x_send.at[0], x_recv.at[0], blk=1 - view)
    swap.start()
    first = push(h_ref.at[view], feat.at[core, view], x_send.at[1], x_recv.at[1], rows=twin)
    first.start()
    feat[core, view] = h_ref[view]
    swap.wait()
    second = push(feat.at[core, 1 - view], feat.at[core, 1 - view], x_send.at[2], x_recv.at[2], rows=twin)
    second.start()
    first.wait()
    second.wait()

    pairs = [(i, j) for i in range(2 * blocks) for j in range(i + 1)][: 2 * blocks]
    for t in range(blocks):
        (i0, j0), (i1, j1) = pairs[t], pairs[blocks + t]
        i, j = i0 + core * (i1 - i0), j0 + core * (j1 - j0)
        per = half_cols // B

        def cols(b):
            return lax.div(b, per), pl.ds(pl.multiple_of(lax.rem(b, per) * B, B), B)

        (hi, ci), (hj, cj) = cols(i), cols(j)
        part[t * B : (t + 1) * B] = (
            mm(feat[0, hi, :, ci], feat[0, hj, :, cj], TN) + mm(feat[1, hi, :, ci], feat[1, hj, :, cj], TN)
        ).astype(jnp.bfloat16)

    def rows_of(p):
        return pl.ds(pl.multiple_of(p * chunk, 16), chunk)

    def scatter(d):
        p = lax.rem(spot + d, peers)
        return push(
            part.at[rows_of(p)], arrived.at[spot], s_send.at[d], s_recv.at[spot], rows=2 * p + core
        )

    def landed(d):
        p = lax.rem(spot + peers - d, peers)
        return push(part.at[rows_of(p)], arrived.at[p], s_send.at[d], s_recv.at[p], rows=2 * p + core)

    lax.fori_loop(1, peers, lambda d, _: (scatter(d).start(), 0)[1], 0)
    mine[...] = part[rows_of(spot)].astype(jnp.float32)

    def add(d, _):
        landed(d).wait_recv()
        mine[...] += arrived[lax.rem(spot + peers - d, peers)].astype(jnp.float32)
        return 0

    lax.fori_loop(1, peers, add, 0)
    mine[...] = mine[...] * (1.0 / total)

    own = pltpu.make_async_copy(mine, cov_ref.at[core, spot], f_send.at[peers])
    own.start()

    def gather(d):
        p = lax.rem(spot + d, peers)
        return push(mine, cov_ref.at[core, spot], g_send.at[d], g_recv.at[spot], rows=2 * p + core)

    def gathered(d):
        p = lax.rem(spot + peers - d, peers)
        return push(mine, cov_ref.at[core, p], g_send.at[d], g_recv.at[p], rows=2 * p + core)

    lax.fori_loop(1, peers, lambda d, _: (gather(d).start(), 0)[1], 0)
    pltpu.make_async_remote_copy(
        src_ref=mine,
        dst_ref=cov_ref.at[core, spot],
        send_sem=f_send.at[0],
        recv_sem=f_recv.at[spot],
        device_id={"rows": twin},
        device_id_type=MESH,
    ).start()

    def forward(d):
        p = lax.rem(spot + peers - d, peers)
        return push(cov_ref.at[core, p], cov_ref.at[core, p], f_send.at[d], f_recv.at[p], rows=twin)

    def pass_on(d, _):
        gathered(d).wait_recv()
        forward(d).start()
        return 0

    lax.fori_loop(1, peers, pass_on, 0)
    own.wait()
    feat_ref[0] = feat[core, 0]
    feat_ref[1] = feat[core, 1]

    def finish(d, _):
        scatter(d).wait_send()
        gather(d).wait_send()
        return 0

    lax.fori_loop(1, peers, finish, 0)

    def settle(d, _):
        p = lax.rem(spot + peers - d, peers)
        done = push(cov_ref.at[core, p], cov_ref.at[1 - core, p], f_send.at[d], f_recv.at[p], rows=twin)
        done.wait_send()
        done.wait_recv()
        return 0

    lax.fori_loop(0, peers, settle, 0)


def covariance(h, peers, total):
    _, rows, half = h.shape
    nb = 2 * half // B
    blocks = nb * (nb + 1) // 4
    chunk = blocks * B // peers
    dma = pltpu.SemaphoreType.DMA
    return pl.pallas_call(
        functools.partial(covariance_kernel, peers, total),
        out_shape=[
            jax.ShapeDtypeStruct((2, rows, half), jnp.bfloat16),
            jax.ShapeDtypeStruct((2, peers, chunk, B), jnp.float32),
        ],
        in_specs=[VMEM],
        out_specs=[VMEM, HBM],
        scratch_shapes=[
            pltpu.VMEM((2, 2, rows, half), jnp.bfloat16),
            pltpu.VMEM((blocks * B, B), jnp.bfloat16),
            pltpu.VMEM((peers, chunk, B), jnp.bfloat16),
            pltpu.VMEM((chunk, B), jnp.float32),
            dma((3,)),
            dma((3,)),
            dma((peers,)),
            dma((peers,)),
            dma((peers,)),
            dma((peers,)),
            dma((peers + 1,)),
            dma((peers,)),
        ],
        compiler_params=pltpu.CompilerParams(collective_id=0, has_side_effects=True, vmem_limit_bytes=56 << 20),
    )(h)


def whiten_block(s_ref, a_ref, m_ref):
    rows=lax.broadcasted_iota(jnp.int32,(B,B),0); cols=lax.broadcasted_iota(jnp.int32,(B,B),1)
    eye=jnp.where(rows==cols,1.0,0.0)
    s=s_ref[...]
    on=jnp.where(rows==cols,s,0.0)
    sc=lax.rsqrt(jnp.sum(on,axis=1,keepdims=True)); sr=lax.rsqrt(jnp.sum(on,axis=0,keepdims=True))
    a=s*sc*sr
    a=jnp.where(rows==cols,1.0,a)
    weight=jnp.where(rows>cols,1.0,jnp.where(rows==cols,0.5,0.0))
    def factor_step(a): return eye-weight*(a-eye)
    t=factor_step(a)
    th=halves(t)
    m_ref[...]=t*sr
    a1=dot3(halves(dot3(th,halves(a),NN)),th,NT)
    a_ref[...]=a1
    def cond(c): return jnp.logical_and(c[0]>1e-3,c[1]<7)
    def body(c):
        a=a_ref[...]
        th=halves(factor_step(a))
        m_ref[...]=dot3(th,halves(m_ref[...]),NN)
        a1=dot3(halves(dot3(th,halves(a),NN)),th,NT)
        a_ref[...]=a1
        return jnp.max(jnp.abs(a1-eye)),c[1]+1
    err,_=lax.while_loop(cond,body,(jnp.max(jnp.abs(a1-eye)),jnp.int32(0)))
    good=err<=1e-3
    @pl.when(good)
    def _():
        th=halves(factor_step(a_ref[...]))
        m_ref[...]=dot3(th,halves(m_ref[...]),NN)
    @pl.when(jnp.logical_not(good))
    def _():
        m_ref[...]=s_ref[...]
        def pivot(j,_):
            s=m_ref[...]
            row=m_ref[pl.ds(j,1),:]
            lane=lax.broadcasted_iota(jnp.int32,(1,B),1)
            p=jnp.sum(jnp.where(lane==j,row,0.0),axis=1,keepdims=True)
            col=jnp.sum(jnp.where(cols==j,s,0.0),axis=1,keepdims=True)
            below=lax.broadcasted_iota(jnp.int32,(B,1),0)>j
            mult=jnp.where(below,col/p,0.0)
            pivot_row=jnp.where(lane==j,1.0,row)
            m_ref[...]=jnp.where(jnp.logical_and(cols==j,below),0.0,s)-mult*pivot_row
            m_ref[pl.ds(j,1),:]=jnp.where(lane<=j,pivot_row,0.0)*lax.rsqrt(p)
            return 0
        lax.fori_loop(0,B,pivot,0)

def factor_kernel(ridge, c_ref, mh_ref, ml_ref, lh, ll, g, xbuf, a_scr, m_scr):
    nb=lh.shape[0]//B
    rows=lax.broadcasted_iota(jnp.int32,(B,B),0); cols=lax.broadcasted_iota(jnp.int32,(B,B),1)
    for k in range(nb):
        kb=slice(k*B,(k+1)*B); done=slice(0,k*B)
        def left(i,_):
            blk=c_ref[i*(i+1)//2+k]
            if k:
                ib=pl.ds(pl.multiple_of(i*B,B),B)
                blk=blk-dot3((lh[ib,done],ll[ib,done]),(lh[kb,done],ll[kb,done]),NT)
            g[i]=blk
            return 0
        lax.fori_loop(k,nb,left,0)
        g[k]=g[k]+jnp.where(rows==cols,ridge,0.0)
        whiten_block(g.at[k],a_scr,m_scr)
        mk=halves(m_scr[...])
        mh_ref[kb,kb],ml_ref[kb,kb]=mk
        if k<nb-1:
            def panel(i,_):
                ib=pl.ds(pl.multiple_of(i*B,B),B)
                mk=mh_ref[kb,kb],ml_ref[kb,kb]
                lh[ib,kb],ll[ib,kb]=halves(dot3(halves(g[i]),mk,NT))
                return 0
            lax.fori_loop(k+1,nb,panel,0)
        for j in range(k):
            jb=slice(j*B,(j+1)*B); span=slice(j*B,k*B)
            x=dot3((lh[kb,span],ll[kb,span]),(mh_ref[span,jb],ml_ref[span,jb]),NN)
            mh_ref[kb,jb],ml_ref[kb,jb]=halves(-dot3(mk,halves(x),NN))

def factor(c,ridge,n):
    return pl.pallas_call(functools.partial(factor_kernel,ridge),
        out_shape=[jax.ShapeDtypeStruct((n,n),jnp.bfloat16)]*2,
        in_specs=[VMEM],out_specs=[VMEM,VMEM],
        scratch_shapes=[pltpu.VMEM((n,n),jnp.bfloat16)]*2+[pltpu.VMEM((n//B,B,B),jnp.float32),pltpu.VMEM((8, 128), jnp.float32)]+[pltpu.VMEM((B,B),jnp.float32)]*2,
        compiler_params=pltpu.CompilerParams(vmem_limit_bytes=60<<20))(c)


def gradient_kernel(feat_ref, mh_ref, ml_ref, text_ref, quant_ref, white, swapped, back, returned, send, recv):
    view = lax.axis_index("blk")
    part = text_ref.shape[0]
    n = mh_ref.shape[0]
    per = feat_ref.shape[2] // B
    barrier = pltpu.get_barrier_semaphore()
    pl.semaphore_signal(barrier, inc=1, device_id={"blk": 1 - view}, device_id_type=MESH)
    pl.semaphore_wait(barrier, 1)

    def exchange(t):
        return push(white.at[t], swapped.at[t], send.at[t], recv.at[t], blk=1 - view)

    give = push(back, returned, send.at[2], recv.at[2], blk=1 - view)

    for t in range(2):
        rows = pl.ds(pl.multiple_of((view + t - 2 * view * t) * part, part), part)
        for j in range(n // B):
            jb = slice(j * B, (j + 1) * B)
            total = jnp.zeros((part, B), jnp.float32)
            for half in range(j // per + 1):
                width = min((j + 1 - half * per) * B, per * B)
                span = slice(half * per * B, half * per * B + width)
                f = feat_ref[half, rows, 0:width]
                total += mm(f, mh_ref[jb, span], NT) + mm(f, ml_ref[jb, span], NT)
            white[t, :, jb] = total.astype(jnp.bfloat16)
        exchange(t).start()

    def gradient(t, j):
        jb = slice(j * B, (j + 1) * B)
        span = slice(j * B, n)
        w = swapped[t, :, span]
        return mm(w, mh_ref[span, jb], NN) + mm(w, ml_ref[span, jb], NN)

    exchange(0).wait()
    for j in range(n // B):
        back[:, j * B : (j + 1) * B] = gradient(0, j).astype(jnp.bfloat16)
    give.start()
    exchange(1).wait()
    own = [text_ref, quant_ref]
    for j in range(n // B):
        jb = slice(j * B, (j + 1) * B)
        value = gradient(1, j)
        text_ref[:, jb] = value
        quant_ref[:, jb] = value
    give.wait()
    theirs = returned[...].astype(jnp.float32)

    @pl.when(view == 0)
    def _():
        quant_ref[...] = theirs

    @pl.when(view == 1)
    def _():
        text_ref[...] = theirs


def gradients(feat, mh, ml):
    _, rows, _ = feat.shape
    n = mh.shape[0]
    part = rows // 2
    dma = pltpu.SemaphoreType.DMA
    return pl.pallas_call(
        gradient_kernel,
        out_shape=[jax.ShapeDtypeStruct((part, n), jnp.float32)] * 2,
        in_specs=[VMEM] * 3,
        out_specs=[VMEM] * 2,
        scratch_shapes=[
            pltpu.VMEM((2, part, n), jnp.bfloat16),
            pltpu.VMEM((2, part, n), jnp.bfloat16),
            pltpu.VMEM((part, n), jnp.bfloat16),
            pltpu.VMEM((part, n), jnp.bfloat16),
            dma((3,)),
            dma((3,)),
        ],
        compiler_params=pltpu.CompilerParams(collective_id=1, has_side_effects=True, vmem_limit_bytes=56 << 20),
    )(feat, mh, ml)


def shards(text_emb, quant_emb, text_head, quant_head):
    peers = lax.axis_size("rows") // 2
    total = text_emb.shape[0] * lax.axis_size("rows")
    h = jnp.stack(
        [
            jnp.dot(text_emb, text_head, preferred_element_type=jnp.float32).astype(jnp.bfloat16),
            jnp.dot(quant_emb, quant_head, preferred_element_type=jnp.float32).astype(jnp.bfloat16),
        ]
    )
    feat, cov = covariance(h, peers, total)
    mh, ml = factor(cov.reshape(-1, B, B), ridge_weight, 2 * h.shape[2])
    return tuple(gradients(feat, mh, ml))


def solution(mesh):
    placed = (P("rows", None), P("rows", None), P(None, "blk"), P(None, "blk"))
    return jax.shard_map(
        shards,
        mesh=mesh,
        in_specs=placed,
        out_specs=(P(("rows", "blk"), None), P(("rows", "blk"), None)),
        check_vma=False,
    )
```

```python
import functools

import jax
import jax.numpy as jnp
from jax import lax
from jax.experimental import pallas as pl
from jax.experimental.pallas import tpu as pltpu
from jax.sharding import PartitionSpec as P

ridge_weight = 0.05
B = 256
NN = (((1,), (0,)), ((), ()))
NT = (((1,), (1,)), ((), ()))
TN = (((0,), (0,)), ((), ()))
MESH = pl.DeviceIdType.MESH
VMEM = pl.BlockSpec(memory_space=pltpu.VMEM)
HBM = pl.BlockSpec(memory_space=pl.ANY)


def mm(a, b, dims):
    return lax.dot_general(a, b, dims, preferred_element_type=jnp.float32)


def halves(x):
    hi = x.astype(jnp.bfloat16)
    return hi, (x - hi.astype(jnp.float32)).astype(jnp.bfloat16)


def dot3(a, b, dims):
    (ah, al), (bh, bl) = a, b
    return mm(ah, bh, dims) + (mm(ah, bl, dims) + mm(al, bh, dims))


def push(src, dst, send, recv, **device):
    return pltpu.make_async_remote_copy(
        src_ref=src, dst_ref=dst, send_sem=send, recv_sem=recv, device_id=device, device_id_type=MESH
    )

SEGMENTS = ((0, 4), (8, 8), (24, 4), (32, 2))


def inverse_factor(s_ref, a_ref, m_ref, bad_ref):
    rows = lax.broadcasted_iota(jnp.int32, (B, B), 0)
    cols = lax.broadcasted_iota(jnp.int32, (B, B), 1)
    eye = jnp.where(rows == cols, 1.0, 0.0)
    weight = jnp.where(rows > cols, 1.0, jnp.where(rows == cols, 0.5, 0.0))
    s = s_ref[...]
    on = jnp.where(rows == cols, s, 0.0)
    sc = lax.rsqrt(jnp.sum(on, axis=1, keepdims=True))
    sr = lax.rsqrt(jnp.sum(on, axis=0, keepdims=True))
    a = jnp.where(rows == cols, 1.0, s * sc * sr)
    step = eye - weight * (a - eye)
    m_ref[...] = step * sr
    a_ref[...] = a
    for turn in range(3):
        t = halves(eye - weight * (a_ref[...] - eye))
        if turn:
            m_ref[...] = dot3(t, halves(m_ref[...]), NN)
        a_ref[...] = dot3(halves(dot3(t, halves(a_ref[...]), NN)), t, NT)
    gap = a_ref[...] - eye
    bad_ref[...] += jnp.where(jnp.sum(gap * gap, axis=0, keepdims=True) <= 2.5e-5, 0.0, 1.0)
    m_ref[...] = dot3(halves(eye - weight * gap), halves(m_ref[...]), NN)


def step_kernel(
    total, ridge, h_ref, text_ref, quant_ref, flag_ref,
    feat, part, arrived, mine, cov, lh, ll, g, a_scr, m_scr, wh, wl, w_send, w_recv, gh, gl, num, back, returned, bad, bad2,
    e_send, e_recv, s_send, s_recv, x_send, x_recv, v_send, v_recv, u_send, u_recv, t_send, t_recv, w_s, w_r, b_s, b_r,
):
    at = lax.axis_index("rows")
    view = lax.axis_index("blk")
    core, xh, y, z = lax.rem(at, 2), lax.rem(at // 2, 2), lax.rem(at // 4, 4), at // 16
    twin = at + 1 - 2 * core
    half_cols = h_ref.shape[2]
    peers = arrived.shape[0]
    nb = lh.shape[0] // B
    per = half_cols // B
    starts = [sum(nb - c for c in range(k)) for k in range(nb)]
    order = [(i, j) for j in range(nb) for i in range(j, nb)]
    u, v = z + core * (y - z), y + core * (z - y)

    def device(p_u, p_v, p_x):
        pz, py = p_u + core * (p_v - p_u), p_v + core * (p_u - p_v)
        return ((pz * 4 + py) * 2 + p_x) * 2 + core

    def device_of(p):
        return device(p // 8, lax.rem(p // 2, 4), lax.rem(p, 2))

    me = (u * 4 + v) * 2 + xh

    barrier = pltpu.get_barrier_semaphore()

    def greet(d, _):
        pl.semaphore_signal(barrier, inc=1, device_id={"rows": device_of(lax.rem(me + d, peers))}, device_id_type=MESH)
        return 0

    lax.fori_loop(1, peers, greet, 0)
    pl.semaphore_signal(barrier, inc=1, device_id={"rows": twin}, device_id_type=MESH)
    pl.semaphore_signal(barrier, inc=1, device_id={"blk": 1 - view}, device_id_type=MESH)
    pl.semaphore_wait(barrier, peers + 1)

    swap = push(h_ref.at[1 - view], feat.at[core, view], e_send.at[0], e_recv.at[0], blk=1 - view)
    swap.start()
    first = push(h_ref.at[view], feat.at[core, view], e_send.at[1], e_recv.at[1], rows=twin)
    first.start()
    feat[core, view] = h_ref[view]
    swap.wait()
    second = push(feat.at[core, 1 - view], feat.at[core, 1 - view], e_send.at[2], e_recv.at[2], rows=twin)
    second.start()
    first.wait()
    second.wait()

    def cols(b):
        return lax.div(b, per), pl.ds(pl.multiple_of(lax.rem(b, per) * B, B), B)

    offset = 0
    spans = []
    for begin, count in SEGMENTS:
        rg = count * B // peers
        spans.append((begin, count, offset, rg))
        for t in range(count):
            (i0, j0), (i1, j1) = order[begin + t], order[begin + count + t]
            (hi, ci), (hj, cj) = cols(i0 + core * (i1 - i0)), cols(j0 + core * (j1 - j0))
            block = mm(feat[0, hi, :, ci], feat[0, hj, :, cj], TN) + mm(feat[1, hi, :, ci], feat[1, hj, :, cj], TN)
            n = B // rg
            part[t * n : (t + 1) * n, offset : offset + rg] = block.astype(jnp.bfloat16).reshape(n, rg, B)
        offset += rg

    def scatter(d):
        p = lax.rem(me + d, peers)
        return push(part.at[p], arrived.at[me], s_send.at[d], s_recv.at[d], rows=device_of(p))

    def landed(d):
        p = lax.rem(me + peers - d, peers)
        return push(part.at[p], arrived.at[p], s_send.at[d], s_recv.at[d], rows=device_of(p))

    lax.fori_loop(1, peers, lambda d, _: (scatter(d).start(), 0)[1], 0)
    mine[...] = part[me].astype(jnp.float32)

    def add(d, _):
        landed(d).wait_recv()
        mine[...] += arrived[lax.rem(me + peers - d, peers)].astype(jnp.float32)
        return 0

    lax.fori_loop(1, peers, add, 0)

    def rows_at(s, c, piece, count):
        begin, size, _, rg = spans[s]
        return pl.ds(pl.multiple_of((begin + c * size) * B + piece * rg, 16), count * rg)

    def same(rows, send, recv, dev):
        return push(cov.at[rows], cov.at[rows], send, recv, rows=dev)

    sent = []
    for s, (begin, size, off, rg) in enumerate(spans):
        cov[rows_at(s, core, me, 1)] = mine[off : off + rg] * (1.0 / total)
        copy = same(rows_at(s, core, me, 1), x_send.at[s], x_recv.at[s], device(u, v, 1 - xh))
        copy.start()
        sent.append(copy)
    other = me + 1 - 2 * xh
    for s in range(len(spans)):
        same(rows_at(s, core, other, 1), x_send.at[s], x_recv.at[s], at).wait_recv()

    def over_v(s, d, pv):
        return same(rows_at(s, core, (u * 4 + pv) * 2, 2), v_send.at[s, d], v_recv.at[s, d], device(u, lax.rem(v + d, 4), xh))

    def over_u(s, d, pu):
        return same(rows_at(s, core, pu * 8, 8), u_send.at[s, d], u_recv.at[s, d], device(lax.rem(u + d, 4), v, xh))

    def to_twin(s, d, c, pu):
        return same(rows_at(s, c, pu * 8, 8), t_send.at[s, d], t_recv.at[s, d], twin)

    for s in range(len(spans)):
        for d in range(1, 4):
            copy = over_v(s, d, v)
            copy.start()
            sent.append(copy)
    for s in range(len(spans)):
        for d in range(1, 4):
            over_v(s, d, lax.rem(v + 4 - d, 4)).wait_recv()
        for d in range(1, 4):
            copy = over_u(s, d, u)
            copy.start()
            sent.append(copy)
        copy = to_twin(s, 0, core, u)
        copy.start()
        sent.append(copy)

    def relay(s):
        for d in range(1, 4):
            pu = lax.rem(u + 4 - d, 4)
            over_u(s, d, pu).wait_recv()
            copy = to_twin(s, d, core, pu)
            copy.start()
            sent.append(copy)

    def ready(s):
        twin_u = y + core * (z - y)
        for d in range(4):
            to_twin(s, d, 1 - core, lax.rem(twin_u + 4 - d, 4)).wait_recv()

    rows = lax.broadcasted_iota(jnp.int32, (B, B), 0)
    lanes = lax.broadcasted_iota(jnp.int32, (B, B), 1)
    bad[...] = jnp.zeros_like(bad)
    relay(0)
    needs = {0: 0, 1: 1, 3: 2, 5: 3}
    for k in range(nb):
        if k in needs:
            ready(needs[k])
        kb, done = slice(k * B, (k + 1) * B), slice(0, k * B)

        def left(i, _):
            value = cov[pl.ds(pl.multiple_of((starts[k] - k + i) * B, B), B)]
            if k:
                ib = pl.ds(pl.multiple_of(i * B, B), B)
                value = value - dot3((lh[ib, done], ll[ib, done]), (lh[kb, done], ll[kb, done]), NT)
            g[i] = value
            return 0

        lax.fori_loop(k, nb, left, 0)
        g[k] = g[k] + jnp.where(rows == lanes, ridge, 0.0)
        inverse_factor(g.at[k], a_scr, m_scr, bad)
        mk = halves(m_scr[...])
        lh[kb, kb], ll[kb, kb] = mk
        if k < 3:
            relay(k + 1)

        def panel(i, _):
            ib = pl.ds(pl.multiple_of(i * B, B), B)
            lh[ib, kb], ll[ib, kb] = halves(dot3(halves(g[i]), (lh[kb, kb], ll[kb, kb]), NT))
            return 0

        if k < nb - 1:
            lax.fori_loop(k + 1, nb, panel, 0)
        f = feat[core, k // per, :, (k % per) * B : (k % per + 1) * B].astype(jnp.float32)
        if k:
            f = f - dot3((wh[:, done], wl[:, done]), (lh[kb, done], ll[kb, done]), NT)
        whi, wlo = halves(dot3(halves(f), mk, NT))
        w_send[k] = whi
        if k < nb - 1:
            wh[:, kb], wl[:, kb] = whi, wlo
        copy = push(w_send.at[k], w_recv.at[k], w_s.at[k], w_r.at[k], blk=1 - view)
        copy.start()
        sent.append(copy)
    flags = push(bad, bad2, w_s.at[nb], w_r.at[nb], blk=1 - view)
    flags.start()

    half = text_ref.shape[0]
    own = pl.ds(pl.multiple_of(view * half, half), half)
    away = pl.ds(pl.multiple_of((1 - view) * half, half), half)
    for k in reversed(range(nb)):
        kb, rest = slice(k * B, (k + 1) * B), slice((k + 1) * B, nb * B)
        push(w_send.at[k], w_recv.at[k], w_s.at[k], w_r.at[k], blk=1 - view).wait_recv()
        value = w_recv[k].astype(jnp.float32)
        if k < nb - 1:
            value = value - dot3((gh[:, rest], gl[:, rest]), (lh[rest, kb], ll[rest, kb]), NN)
        value = dot3(halves(value), (lh[kb, kb], ll[kb, kb]), NN)
        if k:
            gh[:, kb], gl[:, kb] = halves(value)
        num[...] = value
        back[k] = num[away].astype(jnp.bfloat16)
        copy = push(back.at[k], returned.at[k], b_s.at[k], b_r.at[k], blk=1 - view)
        copy.start()
        sent.append(copy)
        text_ref[:, kb] = num[own]
        quant_ref[:, kb] = num[own]
    for k in reversed(range(nb)):
        kb = slice(k * B, (k + 1) * B)
        push(back.at[k], returned.at[k], b_s.at[k], b_r.at[k], blk=1 - view).wait_recv()
        theirs = returned[k].astype(jnp.float32)

        @pl.when(view == 0)
        def _():
            quant_ref[:, kb] = theirs

        @pl.when(view == 1)
        def _():
            text_ref[:, kb] = theirs

    flags.wait()
    flag_ref[...] = bad[...] + bad2[...]
    for copy in sent:
        copy.wait_send()
    lax.fori_loop(1, peers, lambda d, _: (scatter(d).wait_send(), 0)[1], 0)


def whole_step(h, peers, total):
    _, rows, half = h.shape
    n = 2 * half
    nb = n // B
    blocks = nb * (nb + 1) // 4
    chunk = blocks * B // peers
    segs = len(SEGMENTS)
    dma = pltpu.SemaphoreType.DMA
    bf = jnp.bfloat16
    f32 = jnp.float32
    return pl.pallas_call(
        functools.partial(step_kernel, total, ridge_weight),
        out_shape=[jax.ShapeDtypeStruct((rows // 2, n), f32)] * 2 + [jax.ShapeDtypeStruct((8, B), f32)],
        in_specs=[VMEM],
        out_specs=[VMEM] * 3,
        scratch_shapes=[
            pltpu.VMEM((2, 2, rows, half), bf),
            pltpu.VMEM((peers, chunk, B), bf),
            pltpu.VMEM((peers, chunk, B), bf),
            pltpu.VMEM((chunk, B), f32),
            pltpu.VMEM((2 * blocks * B, B), f32),
            pltpu.VMEM((n, n), bf),
            pltpu.VMEM((n, n), bf),
            pltpu.VMEM((nb, B, B), f32),
            pltpu.VMEM((B, B), f32),
            pltpu.VMEM((B, B), f32),
            pltpu.VMEM((rows, n), bf),
            pltpu.VMEM((rows, n), bf),
            pltpu.VMEM((nb, rows, B), bf),
            pltpu.VMEM((nb, rows, B), bf),
            pltpu.VMEM((rows, n), bf),
            pltpu.VMEM((rows, n), bf),
            pltpu.VMEM((rows, B), f32),
            pltpu.VMEM((nb, rows // 2, B), bf),
            pltpu.VMEM((nb, rows // 2, B), bf),
            pltpu.VMEM((8, B), f32),
            pltpu.VMEM((8, B), f32),
            dma((3,)),
            dma((3,)),
            dma((peers,)),
            dma((peers,)),
            dma((segs,)),
            dma((segs,)),
            dma((segs, 4)),
            dma((segs, 4)),
            dma((segs, 4)),
            dma((segs, 4)),
            dma((segs, 4)),
            dma((segs, 4)),
            dma((nb + 1,)),
            dma((nb + 1,)),
            dma((nb,)),
            dma((nb,)),
        ],
        compiler_params=pltpu.CompilerParams(collective_id=0, has_side_effects=True, vmem_limit_bytes=60 << 20),
    )(h)


def direct_kernel(c_ref, m_ref, panel):
    nb = c_ref.shape[0] // B
    rows = lax.broadcasted_iota(jnp.int32, (B, B), 0)
    cols = lax.broadcasted_iota(jnp.int32, (B, B), 1)
    lane = lax.broadcasted_iota(jnp.int32, (1, B), 1)
    sub = lax.broadcasted_iota(jnp.int32, (B, 1), 0)

    def exact(a, b, dims):
        return lax.dot_general(a, b, dims, precision=lax.Precision.HIGHEST, preferred_element_type=jnp.float32)

    def at(i):
        return pl.ds(pl.multiple_of(i * B, B), B)

    def init(i, _):
        def column(j, _):
            m_ref[at(i), at(j)] = jnp.where(j > i, 0.0, c_ref[at(i), at(j)])
            return 0

        return lax.fori_loop(0, nb, column, 0)

    lax.fori_loop(0, nb, init, 0)

    def step(k, _):
        kb = at(k)
        panel[k] = m_ref[kb, kb]

        def pivot(j, _):
            s = panel[k]
            row = panel[k, pl.ds(j, 1), :]
            p = jnp.sum(jnp.where(lane == j, row, 0.0), axis=1, keepdims=True)
            col = jnp.sum(jnp.where(cols == j, s, 0.0), axis=1, keepdims=True)
            below = sub > j
            pivot_row = jnp.where(lane == j, 1.0, row)
            left = jnp.where(jnp.logical_and(cols == j, below), 0.0, s)
            panel[k] = left - jnp.where(below, col / p, 0.0) * pivot_row
            panel[k, pl.ds(j, 1), :] = jnp.where(lane <= j, pivot_row, 0.0) * lax.rsqrt(p)
            return 0

        lax.fori_loop(0, B, pivot, 0)
        m_ref[kb, kb] = panel[k]

        def inverse_row(j, _):
            m_ref[kb, at(j)] = exact(m_ref[kb, kb], m_ref[kb, at(j)], NN)
            return 0

        lax.fori_loop(0, k, inverse_row, 0)

        def factor(i, _):
            panel[i] = exact(m_ref[at(i), kb], m_ref[kb, kb], NT)
            m_ref[at(i), kb] = jnp.zeros((B, B), jnp.float32)
            return 0

        lax.fori_loop(k + 1, nb, factor, 0)

        def update(i, _):
            def inverse_part(j, _):
                m_ref[at(i), at(j)] = m_ref[at(i), at(j)] - exact(panel[i], m_ref[kb, at(j)], NN)
                return 0

            lax.fori_loop(0, k + 1, inverse_part, 0)

            def schur(j, _):
                m_ref[at(i), at(j)] = m_ref[at(i), at(j)] - exact(panel[i], panel[j], NT)
                return 0

            return lax.fori_loop(k + 1, i + 1, schur, 0)

        return lax.fori_loop(k + 1, nb, update, 0)

    lax.fori_loop(0, nb, step, 0)


def direct_step(h, total):
    view = lax.axis_index("blk")
    full = lax.all_gather(h, "blk", axis=2, tiled=True)
    feat = lax.dynamic_index_in_dim(full, view, 0, keepdims=False)
    n = feat.shape[1]
    cov = lax.psum(mm(feat, feat, TN), "rows") / total + ridge_weight * jnp.eye(n, dtype=jnp.float32)
    inverse = pl.pallas_call(
        direct_kernel,
        out_shape=jax.ShapeDtypeStruct((n, n), jnp.float32),
        in_specs=[VMEM],
        out_specs=VMEM,
        scratch_shapes=[pltpu.VMEM((n // B, B, B), jnp.float32)],
        compiler_params=pltpu.CompilerParams(vmem_limit_bytes=56 << 20),
    )(cov)
    exact = functools.partial(
        lax.dot_general, precision=lax.Precision.HIGHEST, preferred_element_type=jnp.float32
    )
    white = lax.ppermute(exact(feat.astype(jnp.float32), inverse, NT), "blk", [(0, 1), (1, 0)])
    grad = exact(white, inverse, NN)
    placed = lax.all_to_all(grad[None], "blk", split_axis=1, concat_axis=0, tiled=True)
    return placed[0], placed[1]


def shards(text_emb, quant_emb, text_head, quant_head):
    peers = lax.axis_size("rows") // 2
    total = text_emb.shape[0] * lax.axis_size("rows")
    h = jnp.stack(
        [
            jnp.dot(text_emb, text_head, preferred_element_type=jnp.float32).astype(jnp.bfloat16),
            jnp.dot(quant_emb, quant_head, preferred_element_type=jnp.float32).astype(jnp.bfloat16),
        ]
    )
    text, quant, flag = whole_step(h, peers, total)
    return lax.cond(jnp.max(flag) > 0, lambda: direct_step(h, total), lambda: (text, quant))


def solution(mesh):
    placed = (P("rows", None), P("rows", None), P(None, "blk"), P(None, "blk"))
    return jax.shard_map(
        shards,
        mesh=mesh,
        in_specs=placed,
        out_specs=(P(("rows", "blk"), None), P(("rows", "blk"), None)),
        check_vma=False,
    )
```

```python
import functools

import jax
import jax.numpy as jnp
from jax import lax
from jax.experimental import pallas as pl
from jax.experimental.pallas import tpu as pltpu
from jax.sharding import PartitionSpec as P

ridge_weight = 0.05
B = 256
NN = (((1,), (0,)), ((), ()))
NT = (((1,), (1,)), ((), ()))
TN = (((0,), (0,)), ((), ()))
MESH = pl.DeviceIdType.MESH
VMEM = pl.BlockSpec(memory_space=pltpu.VMEM)
HBM = pl.BlockSpec(memory_space=pl.ANY)


def mm(a, b, dims):
    return lax.dot_general(a, b, dims, preferred_element_type=jnp.float32)


def halves(x):
    hi = x.astype(jnp.bfloat16)
    return hi, (x - hi.astype(jnp.float32)).astype(jnp.bfloat16)


def dot3(a, b, dims):
    (ah, al), (bh, bl) = a, b
    return mm(ah, bh, dims) + (mm(ah, bl, dims) + mm(al, bh, dims))


def push(src, dst, send, recv, **device):
    return pltpu.make_async_remote_copy(
        src_ref=src, dst_ref=dst, send_sem=send, recv_sem=recv, device_id=device, device_id_type=MESH
    )

SEGMENTS = ((0, 4), (8, 4), (16, 4), (24, 4), (32, 2))
EARLY = 2


def inverse_factor(s_ref, a_ref, m_ref, bad_ref):
    rows = lax.broadcasted_iota(jnp.int32, (B, B), 0)
    cols = lax.broadcasted_iota(jnp.int32, (B, B), 1)
    eye = jnp.where(rows == cols, 1.0, 0.0)
    weight = jnp.where(rows > cols, 1.0, jnp.where(rows == cols, 0.5, 0.0))
    s = s_ref[...]
    on = jnp.where(rows == cols, s, 0.0)
    sc = lax.rsqrt(jnp.sum(on, axis=1, keepdims=True))
    sr = lax.rsqrt(jnp.sum(on, axis=0, keepdims=True))
    a = jnp.where(rows == cols, 1.0, s * sc * sr)
    step = eye - weight * (a - eye)
    m_ref[...] = step * sr
    a_ref[...] = a
    for turn in range(3):
        t = halves(eye - weight * (a_ref[...] - eye))
        if turn:
            m_ref[...] = dot3(t, halves(m_ref[...]), NN)
        a_ref[...] = dot3(halves(dot3(t, halves(a_ref[...]), NN)), t, NT)
    gap = a_ref[...] - eye
    bad_ref[...] += jnp.where(jnp.sum(gap * gap, axis=0, keepdims=True) <= 2.5e-5, 0.0, 1.0)
    m_ref[...] = dot3(halves(eye - weight * gap), halves(m_ref[...]), NN)


def step_kernel(
    total, ridge, h_ref, text_ref, quant_ref, flag_ref,
    feat, part, arrived, mine, cov, lh, ll, g, a_scr, m_scr, wh, wl, w_send, w_recv, gh, gl, num, back, returned, bad, bad2,
    e_send, e_recv, s_send, s_recv, x_send, x_recv, v_send, v_recv, u_send, u_recv, t_send, t_recv, w_s, w_r, b_s, b_r,
):
    at = lax.axis_index("rows")
    view = lax.axis_index("blk")
    core, xh, y, z = lax.rem(at, 2), lax.rem(at // 2, 2), lax.rem(at // 4, 4), at // 16
    twin = at + 1 - 2 * core
    half_cols = h_ref.shape[2]
    peers = arrived.shape[0]
    nb = lh.shape[0] // B
    per = half_cols // B
    starts = [sum(nb - c for c in range(k)) for k in range(nb)]
    order = [(i, j) for j in range(nb) for i in range(j, nb)]
    u, v = z + core * (y - z), y + core * (z - y)

    def device(p_u, p_v, p_x):
        pz, py = p_u + core * (p_v - p_u), p_v + core * (p_u - p_v)
        return ((pz * 4 + py) * 2 + p_x) * 2 + core

    def device_of(p):
        return device(p // 8, lax.rem(p // 2, 4), lax.rem(p, 2))

    me = (u * 4 + v) * 2 + xh

    barrier = pltpu.get_barrier_semaphore()

    def greet(d, _):
        pl.semaphore_signal(barrier, inc=1, device_id={"rows": device_of(lax.rem(me + d, peers))}, device_id_type=MESH)
        return 0

    lax.fori_loop(1, peers, greet, 0)
    pl.semaphore_signal(barrier, inc=1, device_id={"rows": twin}, device_id_type=MESH)
    pl.semaphore_signal(barrier, inc=1, device_id={"blk": 1 - view}, device_id_type=MESH)
    pl.semaphore_wait(barrier, peers + 1)

    swap = push(h_ref.at[1 - view], feat.at[core, view], e_send.at[0], e_recv.at[0], blk=1 - view)
    swap.start()
    first = push(h_ref.at[view], feat.at[core, view], e_send.at[1], e_recv.at[1], rows=twin)
    first.start()
    feat[core, view] = h_ref[view]
    swap.wait()
    second = push(feat.at[core, 1 - view], feat.at[core, 1 - view], e_send.at[2], e_recv.at[2], rows=twin)
    second.start()
    first.wait()
    second.wait()

    def cols(b):
        return lax.div(b, per), pl.ds(pl.multiple_of(lax.rem(b, per) * B, B), B)

    offset = 0
    spans = []
    for begin, count in SEGMENTS:
        rg = count * B // peers
        spans.append((begin, count, offset, rg))
        for t in range(count):
            (i0, j0), (i1, j1) = order[begin + t], order[begin + count + t]
            (hi, ci), (hj, cj) = cols(i0 + core * (i1 - i0)), cols(j0 + core * (j1 - j0))
            block = mm(feat[0, hi, :, ci], feat[0, hj, :, cj], TN) + mm(feat[1, hi, :, ci], feat[1, hj, :, cj], TN)
            n = B // rg
            part[t * n : (t + 1) * n, offset : offset + rg] = block.astype(jnp.bfloat16).reshape(n, rg, B)
        offset += rg

    cut = spans[EARLY][2]
    waves = [(0, cut), (cut, mine.shape[0] - cut)]

    def scatter(w, d):
        p = lax.rem(me + d, peers)
        piece = pl.ds(*waves[w])
        return push(part.at[p, piece], arrived.at[me, piece], s_send.at[w, d], s_recv.at[w, d], rows=device_of(p))

    def landed(w, d):
        p = lax.rem(me + peers - d, peers)
        piece = pl.ds(*waves[w])
        return push(part.at[p, piece], arrived.at[p, piece], s_send.at[w, d], s_recv.at[w, d], rows=device_of(p))

    for w in range(2):
        lax.fori_loop(1, peers, lambda d, _: (scatter(w, d).start(), 0)[1], 0)

    def reduce(w):
        piece = pl.ds(*waves[w])
        mine[piece] = part[me, piece].astype(jnp.float32)

        def add(d, _):
            landed(w, d).wait_recv()
            mine[piece] += arrived[lax.rem(me + peers - d, peers), piece].astype(jnp.float32)
            return 0

        lax.fori_loop(1, peers, add, 0)

    def rows_at(s, c, piece, count):
        begin, size, _, rg = spans[s]
        return pl.ds(pl.multiple_of((begin + c * size) * B + piece * rg, 16), count * rg)

    def same(rows, send, recv, dev):
        return push(cov.at[rows], cov.at[rows], send, recv, rows=dev)

    sent = []

    def go(copy):
        copy.start()
        sent.append(copy)

    def over_x(s, piece):
        return same(rows_at(s, core, piece, 1), x_send.at[s], x_recv.at[s], device(u, v, 1 - xh))

    def over_v(s, d, pv):
        return same(rows_at(s, core, (u * 4 + pv) * 2, 2), v_send.at[s, d], v_recv.at[s, d], device(u, lax.rem(v + d, 4), xh))

    def over_u(s, d, pu):
        return same(rows_at(s, core, pu * 8, 8), u_send.at[s, d], u_recv.at[s, d], device(lax.rem(u + d, 4), v, xh))

    def to_twin(s, d, c, pu):
        return same(rows_at(s, c, pu * 8, 8), t_send.at[s, d], t_recv.at[s, d], twin)

    def near(segments):
        for s in segments:
            _, _, off, rg = spans[s]
            cov[rows_at(s, core, me, 1)] = mine[off : off + rg] * (1.0 / total)
            go(over_x(s, me))

    def middle(segments):
        for s in segments:
            over_x(s, me + 1 - 2 * xh).wait_recv()
            for d in range(1, 4):
                go(over_v(s, d, v))

    def far(segments):
        for s in segments:
            for d in range(1, 4):
                over_v(s, d, lax.rem(v + 4 - d, 4)).wait_recv()
            for d in range(1, 4):
                go(over_u(s, d, u))
            go(to_twin(s, 0, core, u))

    def relay(s):
        for d in range(1, 4):
            pu = lax.rem(u + 4 - d, 4)
            over_u(s, d, pu).wait_recv()
            go(to_twin(s, d, core, pu))

    def ready(s):
        twin_u = y + core * (z - y)
        for d in range(4):
            to_twin(s, d, 1 - core, lax.rem(twin_u + 4 - d, 4)).wait_recv()

    rows = lax.broadcasted_iota(jnp.int32, (B, B), 0)
    lanes = lax.broadcasted_iota(jnp.int32, (B, B), 1)
    bad[...] = jnp.zeros_like(bad)
    early, late = range(EARLY), range(EARLY, len(spans))
    reduce(0)
    near(early)
    middle(early)
    far(early)
    reduce(1)
    near(late)
    middle(late)
    relay(0)
    far(late)
    needs = {0: 0, 1: 1, 2: 2, 3: 3, 5: 4}
    for k in range(nb):
        if k in needs:
            ready(needs[k])
        kb, done = slice(k * B, (k + 1) * B), slice(0, k * B)

        def left(i, _):
            value = cov[pl.ds(pl.multiple_of((starts[k] - k + i) * B, B), B)]
            if k:
                ib = pl.ds(pl.multiple_of(i * B, B), B)
                value = value - dot3((lh[ib, done], ll[ib, done]), (lh[kb, done], ll[kb, done]), NT)
            g[i] = value
            return 0

        lax.fori_loop(k, nb, left, 0)
        g[k] = g[k] + jnp.where(rows == lanes, ridge, 0.0)
        inverse_factor(g.at[k], a_scr, m_scr, bad)
        mk = halves(m_scr[...])
        lh[kb, kb], ll[kb, kb] = mk
        if k + 1 < len(spans):
            relay(k + 1)

        def panel(i, _):
            ib = pl.ds(pl.multiple_of(i * B, B), B)
            lh[ib, kb], ll[ib, kb] = halves(dot3(halves(g[i]), (lh[kb, kb], ll[kb, kb]), NT))
            return 0

        if k < nb - 1:
            lax.fori_loop(k + 1, nb, panel, 0)
        f = feat[core, k // per, :, (k % per) * B : (k % per + 1) * B].astype(jnp.float32)
        if k:
            f = f - dot3((wh[:, done], wl[:, done]), (lh[kb, done], ll[kb, done]), NT)
        whi, wlo = halves(dot3(halves(f), mk, NT))
        w_send[k] = whi
        if k < nb - 1:
            wh[:, kb], wl[:, kb] = whi, wlo
        go(push(w_send.at[k], w_recv.at[k], w_s.at[k], w_r.at[k], blk=1 - view))
    flags = push(bad, bad2, w_s.at[nb], w_r.at[nb], blk=1 - view)
    flags.start()

    half = text_ref.shape[0]
    own = pl.ds(pl.multiple_of(view * half, half), half)
    away = pl.ds(pl.multiple_of((1 - view) * half, half), half)
    for k in reversed(range(nb)):
        kb, rest = slice(k * B, (k + 1) * B), slice((k + 1) * B, nb * B)
        push(w_send.at[k], w_recv.at[k], w_s.at[k], w_r.at[k], blk=1 - view).wait_recv()
        value = w_recv[k].astype(jnp.float32)
        if k < nb - 1:
            value = value - dot3((gh[:, rest], gl[:, rest]), (lh[rest, kb], ll[rest, kb]), NN)
        value = dot3(halves(value), (lh[kb, kb], ll[kb, kb]), NN)
        if k:
            gh[:, kb], gl[:, kb] = halves(value)
        num[...] = value
        back[k] = num[away].astype(jnp.bfloat16)
        go(push(back.at[k], returned.at[k], b_s.at[k], b_r.at[k], blk=1 - view))
        text_ref[:, kb] = num[own]
        quant_ref[:, kb] = num[own]
    for k in reversed(range(nb)):
        kb = slice(k * B, (k + 1) * B)
        push(back.at[k], returned.at[k], b_s.at[k], b_r.at[k], blk=1 - view).wait_recv()
        theirs = returned[k].astype(jnp.float32)

        @pl.when(view == 0)
        def _():
            quant_ref[:, kb] = theirs

        @pl.when(view == 1)
        def _():
            text_ref[:, kb] = theirs

    flags.wait()
    flag_ref[0] = jnp.sum(bad[...] + bad2[...])
    for copy in sent:
        copy.wait_send()
    for w in range(2):
        lax.fori_loop(1, peers, lambda d, _: (scatter(w, d).wait_send(), 0)[1], 0)


def whole_step(h, peers, total):
    _, rows, half = h.shape
    n = 2 * half
    nb = n // B
    blocks = nb * (nb + 1) // 4
    chunk = blocks * B // peers
    segs = len(SEGMENTS)
    dma = pltpu.SemaphoreType.DMA
    bf = jnp.bfloat16
    f32 = jnp.float32
    return pl.pallas_call(
        functools.partial(step_kernel, total, ridge_weight),
        out_shape=[jax.ShapeDtypeStruct((rows // 2, n), f32)] * 2 + [jax.ShapeDtypeStruct((1,), f32)],
        in_specs=[VMEM],
        out_specs=[VMEM] * 2 + [pl.BlockSpec(memory_space=pltpu.SMEM)],
        scratch_shapes=[
            pltpu.VMEM((2, 2, rows, half), bf),
            pltpu.VMEM((peers, chunk, B), bf),
            pltpu.VMEM((peers, chunk, B), bf),
            pltpu.VMEM((chunk, B), f32),
            pltpu.VMEM((2 * blocks * B, B), f32),
            pltpu.VMEM((n, n), bf),
            pltpu.VMEM((n, n), bf),
            pltpu.VMEM((nb, B, B), f32),
            pltpu.VMEM((B, B), f32),
            pltpu.VMEM((B, B), f32),
            pltpu.VMEM((rows, n), bf),
            pltpu.VMEM((rows, n), bf),
            pltpu.VMEM((nb, rows, B), bf),
            pltpu.VMEM((nb, rows, B), bf),
            pltpu.VMEM((rows, n), bf),
            pltpu.VMEM((rows, n), bf),
            pltpu.VMEM((rows, B), f32),
            pltpu.VMEM((nb, rows // 2, B), bf),
            pltpu.VMEM((nb, rows // 2, B), bf),
            pltpu.VMEM((8, B), f32),
            pltpu.VMEM((8, B), f32),
            dma((3,)),
            dma((3,)),
            dma((2, peers)),
            dma((2, peers)),
            dma((segs,)),
            dma((segs,)),
            dma((segs, 4)),
            dma((segs, 4)),
            dma((segs, 4)),
            dma((segs, 4)),
            dma((segs, 4)),
            dma((segs, 4)),
            dma((nb + 1,)),
            dma((nb + 1,)),
            dma((nb,)),
            dma((nb,)),
        ],
        compiler_params=pltpu.CompilerParams(collective_id=0, has_side_effects=True, vmem_limit_bytes=60 << 20),
    )(h)


def direct_kernel(c_ref, m_ref, panel):
    nb = c_ref.shape[0] // B
    rows = lax.broadcasted_iota(jnp.int32, (B, B), 0)
    cols = lax.broadcasted_iota(jnp.int32, (B, B), 1)
    lane = lax.broadcasted_iota(jnp.int32, (1, B), 1)
    sub = lax.broadcasted_iota(jnp.int32, (B, 1), 0)

    def exact(a, b, dims):
        return lax.dot_general(a, b, dims, precision=lax.Precision.HIGHEST, preferred_element_type=jnp.float32)

    def at(i):
        return pl.ds(pl.multiple_of(i * B, B), B)

    def init(i, _):
        def column(j, _):
            m_ref[at(i), at(j)] = jnp.where(j > i, 0.0, c_ref[at(i), at(j)])
            return 0

        return lax.fori_loop(0, nb, column, 0)

    lax.fori_loop(0, nb, init, 0)

    def step(k, _):
        kb = at(k)
        panel[k] = m_ref[kb, kb]

        def pivot(j, _):
            s = panel[k]
            row = panel[k, pl.ds(j, 1), :]
            p = jnp.sum(jnp.where(lane == j, row, 0.0), axis=1, keepdims=True)
            col = jnp.sum(jnp.where(cols == j, s, 0.0), axis=1, keepdims=True)
            below = sub > j
            pivot_row = jnp.where(lane == j, 1.0, row)
            left = jnp.where(jnp.logical_and(cols == j, below), 0.0, s)
            panel[k] = left - jnp.where(below, col / p, 0.0) * pivot_row
            panel[k, pl.ds(j, 1), :] = jnp.where(lane <= j, pivot_row, 0.0) * lax.rsqrt(p)
            return 0

        lax.fori_loop(0, B, pivot, 0)
        m_ref[kb, kb] = panel[k]

        def inverse_row(j, _):
            m_ref[kb, at(j)] = exact(m_ref[kb, kb], m_ref[kb, at(j)], NN)
            return 0

        lax.fori_loop(0, k, inverse_row, 0)

        def factor(i, _):
            panel[i] = exact(m_ref[at(i), kb], m_ref[kb, kb], NT)
            m_ref[at(i), kb] = jnp.zeros((B, B), jnp.float32)
            return 0

        lax.fori_loop(k + 1, nb, factor, 0)

        def update(i, _):
            def inverse_part(j, _):
                m_ref[at(i), at(j)] = m_ref[at(i), at(j)] - exact(panel[i], m_ref[kb, at(j)], NN)
                return 0

            lax.fori_loop(0, k + 1, inverse_part, 0)

            def schur(j, _):
                m_ref[at(i), at(j)] = m_ref[at(i), at(j)] - exact(panel[i], panel[j], NT)
                return 0

            return lax.fori_loop(k + 1, i + 1, schur, 0)

        return lax.fori_loop(k + 1, nb, update, 0)

    lax.fori_loop(0, nb, step, 0)


def direct_step(h, total):
    view = lax.axis_index("blk")
    ranks = lax.axis_size("rows")

    def swapped(x):
        return lax.ppermute(x, "blk", [(0, 1), (1, 0)])

    near = lax.dynamic_index_in_dim(h, view, 0, keepdims=False)
    far = swapped(lax.dynamic_index_in_dim(h, 1 - view, 0, keepdims=False))
    feat = jnp.where(view == 0, jnp.concatenate([near, far], 1), jnp.concatenate([far, near], 1))
    n = feat.shape[1]
    cov = mm(feat, feat, TN)
    hop = 1
    while hop < ranks:
        cov = cov + lax.ppermute(cov, "rows", [(r, r ^ hop) for r in range(ranks)])
        hop *= 2
    cov = cov / total + ridge_weight * jnp.eye(n, dtype=jnp.float32)
    inverse = pl.pallas_call(
        direct_kernel,
        out_shape=jax.ShapeDtypeStruct((n, n), jnp.float32),
        in_specs=[VMEM],
        out_specs=VMEM,
        scratch_shapes=[pltpu.VMEM((n // B, B, B), jnp.float32)],
        compiler_params=pltpu.CompilerParams(vmem_limit_bytes=56 << 20),
    )(cov)
    exact = functools.partial(
        lax.dot_general, precision=lax.Precision.HIGHEST, preferred_element_type=jnp.float32
    )
    white = swapped(exact(feat.astype(jnp.float32), inverse, NT))
    grad = exact(white, inverse, NN)
    half = grad.shape[0] // 2
    own = lax.dynamic_slice_in_dim(grad, view * half, half, 0)
    other = swapped(lax.dynamic_slice_in_dim(grad, (1 - view) * half, half, 0))
    return jnp.where(view == 0, own, other), jnp.where(view == 0, other, own)


def shards(text_emb, quant_emb, text_head, quant_head):
    peers = lax.axis_size("rows") // 2
    total = text_emb.shape[0] * lax.axis_size("rows")
    h = jnp.stack(
        [
            jnp.dot(text_emb, text_head, preferred_element_type=jnp.float32).astype(jnp.bfloat16),
            jnp.dot(quant_emb, quant_head, preferred_element_type=jnp.float32).astype(jnp.bfloat16),
        ]
    )
    text, quant, flag = whole_step(h, peers, total)
    return lax.cond(flag[0] > 0, lambda: direct_step(h, total), lambda: (text, quant))


def solution(mesh):
    placed = (P("rows", None), P("rows", None), P(None, "blk"), P(None, "blk"))
    return jax.shard_map(
        shards,
        mesh=mesh,
        in_specs=placed,
        out_specs=(P(("rows", "blk"), None), P(("rows", "blk"), None)),
        check_vma=False,
    )
```

```python
import functools

import jax
import jax.numpy as jnp
from jax import lax
from jax.experimental import pallas as pl
from jax.experimental.pallas import tpu as pltpu
from jax.sharding import PartitionSpec as P

ridge_weight = 0.05
B = 256
NN = (((1,), (0,)), ((), ()))
NT = (((1,), (1,)), ((), ()))
TN = (((0,), (0,)), ((), ()))
MESH = pl.DeviceIdType.MESH
VMEM = pl.BlockSpec(memory_space=pltpu.VMEM)
HBM = pl.BlockSpec(memory_space=pl.ANY)


def mm(a, b, dims):
    return lax.dot_general(a, b, dims, preferred_element_type=jnp.float32)


def halves(x):
    hi = x.astype(jnp.bfloat16)
    return hi, (x - hi.astype(jnp.float32)).astype(jnp.bfloat16)


def dot3(a, b, dims):
    (ah, al), (bh, bl) = a, b
    return mm(ah, bh, dims) + (mm(ah, bl, dims) + mm(al, bh, dims))


def push(src, dst, send, recv, **device):
    return pltpu.make_async_remote_copy(
        src_ref=src, dst_ref=dst, send_sem=send, recv_sem=recv, device_id=device, device_id_type=MESH
    )

SEGMENTS = ((0, 4), (8, 4), (16, 4), (24, 4), (32, 2))
EARLY = 2


def inverse_factor(s_ref, a_ref, m_ref, bad_ref):
    rows = lax.broadcasted_iota(jnp.int32, (B, B), 0)
    cols = lax.broadcasted_iota(jnp.int32, (B, B), 1)
    eye = jnp.where(rows == cols, 1.0, 0.0)
    weight = jnp.where(rows > cols, 1.0, jnp.where(rows == cols, 0.5, 0.0))
    s = s_ref[...]
    on = jnp.where(rows == cols, s, 0.0)
    sc = lax.rsqrt(jnp.sum(on, axis=1, keepdims=True))
    sr = lax.rsqrt(jnp.sum(on, axis=0, keepdims=True))
    a = jnp.where(rows == cols, 1.0, s * sc * sr)
    step = eye - weight * (a - eye)
    m_ref[...] = step * sr
    a_ref[...] = a
    for turn in range(3):
        t = halves(eye - weight * (a_ref[...] - eye))
        if turn:
            m_ref[...] = dot3(t, halves(m_ref[...]), NN)
        a_ref[...] = dot3(halves(dot3(t, halves(a_ref[...]), NN)), t, NT)
    gap = a_ref[...] - eye
    bad_ref[...] += jnp.where(jnp.sum(gap * gap, axis=0, keepdims=True) <= 2.5e-5, 0.0, 1.0)
    m_ref[...] = dot3(halves(eye - weight * gap), halves(m_ref[...]), NN)


def step_kernel(
    total, ridge, text_emb, quant_emb, text_head, quant_head, text_ref, quant_ref, flag_ref,
    feat, away_feat, part, arrived, mine, cov, lh, ll, g, a_scr, m_scr, wh, wl, w_send, w_recv, gh, gl, num, back, returned, bad, bad2,
    h_sem, e_send, e_recv, s_send, s_recv, x_send, x_recv, v_send, v_recv, u_send, u_recv, t_send, t_recv, w_s, w_r, b_s, b_r,
):
    at = lax.axis_index("rows")
    view = lax.axis_index("blk")
    core, xh, y, z = lax.rem(at, 2), lax.rem(at // 2, 2), lax.rem(at // 4, 4), at // 16
    twin = at + 1 - 2 * core
    peers = arrived.shape[0]
    nb = lh.shape[0] // B
    per = nb // 2
    starts = [sum(nb - c for c in range(k)) for k in range(nb)]
    order = [(i, j) for j in range(nb) for i in range(j, nb)]
    u, v = z + core * (y - z), y + core * (z - y)

    def device(p_u, p_v, p_x):
        pz, py = p_u + core * (p_v - p_u), p_v + core * (p_u - p_v)
        return ((pz * 4 + py) * 2 + p_x) * 2 + core

    def device_of(p):
        return device(p // 8, lax.rem(p // 2, 4), lax.rem(p, 2))

    me = (u * 4 + v) * 2 + xh

    depth = text_emb.shape[1] // 2
    places = ((wh, wl, lh), (gh, gl, ll))

    def for_view(which, text, quant):
        @pl.when(view == 1 - which)
        def _():
            text()

        @pl.when(view == which)
        def _():
            quant()

    def emb_copy(src, which, half):
        part_of = src.at[:, half * depth : (half + 1) * depth]
        return pltpu.make_async_copy(part_of, places[which][half], h_sem.at[which, 2 * per + half])

    def head_copy(src, which, half, c):
        part_of = src.at[half * depth : (half + 1) * depth, c * B : (c + 1) * B]
        at_cols = slice((half * per + c) * B, (half * per + c + 1) * B)
        return pltpu.make_async_copy(part_of, places[which][2].at[:, at_cols], h_sem.at[which, 2 * c + half])

    def fetch(which, emb, head):
        for half in range(2):
            emb_copy(emb, which, half).start()
        for c in range(per):
            for half in range(2):
                head_copy(head, which, half, c).start()

    for which in range(2):
        for_view(which, lambda: fetch(which, text_emb, text_head), lambda: fetch(which, quant_emb, quant_head))

    barrier = pltpu.get_barrier_semaphore()

    def greet(d, _):
        pl.semaphore_signal(barrier, inc=1, device_id={"rows": device_of(lax.rem(me + d, peers))}, device_id_type=MESH)
        return 0

    pl.semaphore_signal(barrier, inc=1, device_id={"blk": 1 - view}, device_id_type=MESH)
    pl.semaphore_signal(barrier, inc=1, device_id={"rows": twin}, device_id_type=MESH)
    lax.fori_loop(1, peers, greet, 0)

    def project(which, c):
        emb0, emb1, head = places[which]
        for half in range(2):
            head_copy(text_head, which, half, c).wait()
        lo, hi = slice(c * B, (c + 1) * B), slice((per + c) * B, (per + c + 1) * B)
        return (mm(emb0[...], head[:, lo], NN) + mm(emb1[...], head[:, hi], NN)).astype(jnp.bfloat16)

    sent = []

    def go(copy):
        copy.start()
        sent.append(copy)

    def swap(c, which_view):
        return push(away_feat.at[c], feat.at[core, which_view * per + c], e_send.at[0, c], e_recv.at[0, c], blk=1 - view)

    def share(turn, which_core, b):
        c = lax.rem(b, per)
        block = feat.at[which_core, b]
        return push(block, block, e_send.at[turn, c], e_recv.at[turn, c], rows=twin)

    for which in range(2):
        for half in range(2):
            emb_copy(text_emb, which, half).wait()
        for c in range(per):
            if which == 0:
                away_feat[c] = project(which, c)
                if c == 0:
                    pl.semaphore_wait(barrier, peers + 1)
                go(swap(c, view))
            else:
                feat[core, view * per + c] = project(which, c)
                go(share(1, core, view * per + c))
    for c in range(per):
        swap(c, 1 - view).wait_recv()
        go(share(2, core, (1 - view) * per + c))
    for c in range(per):
        share(1, 1 - core, view * per + c).wait_recv()
    for c in range(per):
        share(2, 1 - core, (1 - view) * per + c).wait_recv()

    offset = 0
    spans = []
    for begin, count in SEGMENTS:
        rg = count * B // peers
        spans.append((begin, count, offset, rg))
        for t in range(count):
            (i0, j0), (i1, j1) = order[begin + t], order[begin + count + t]
            i, j = i0 + core * (i1 - i0), j0 + core * (j1 - j0)
            block = mm(feat[0, i], feat[0, j], TN) + mm(feat[1, i], feat[1, j], TN)
            n = B // rg
            part[t * n : (t + 1) * n, offset : offset + rg] = block.astype(jnp.bfloat16).reshape(n, rg, B)
        offset += rg

    cut = spans[EARLY][2]
    waves = [(0, cut), (cut, mine.shape[0] - cut)]

    def scatter(w, d):
        p = lax.rem(me + d, peers)
        piece = pl.ds(*waves[w])
        return push(part.at[p, piece], arrived.at[me, piece], s_send.at[w, d], s_recv.at[w, d], rows=device_of(p))

    def landed(w, d):
        p = lax.rem(me + peers - d, peers)
        piece = pl.ds(*waves[w])
        return push(part.at[p, piece], arrived.at[p, piece], s_send.at[w, d], s_recv.at[w, d], rows=device_of(p))

    for w in range(2):
        lax.fori_loop(1, peers, lambda d, _: (scatter(w, d).start(), 0)[1], 0)

    def reduce(w):
        piece = pl.ds(*waves[w])
        mine[piece] = part[me, piece].astype(jnp.float32)

        def add(d, _):
            landed(w, d).wait_recv()
            mine[piece] += arrived[lax.rem(me + peers - d, peers), piece].astype(jnp.float32)
            return 0

        lax.fori_loop(1, peers, add, 0)

    def rows_at(s, c, piece, count):
        begin, size, _, rg = spans[s]
        return pl.ds(pl.multiple_of((begin + c * size) * B + piece * rg, 16), count * rg)

    def same(rows, send, recv, dev):
        return push(cov.at[rows], cov.at[rows], send, recv, rows=dev)

    def over_x(s, piece):
        return same(rows_at(s, core, piece, 1), x_send.at[s], x_recv.at[s], device(u, v, 1 - xh))

    def over_v(s, d, pv):
        return same(rows_at(s, core, (u * 4 + pv) * 2, 2), v_send.at[s, d], v_recv.at[s, d], device(u, lax.rem(v + d, 4), xh))

    def over_u(s, d, pu):
        return same(rows_at(s, core, pu * 8, 8), u_send.at[s, d], u_recv.at[s, d], device(lax.rem(u + d, 4), v, xh))

    def to_twin(s, d, c, pu):
        return same(rows_at(s, c, pu * 8, 8), t_send.at[s, d], t_recv.at[s, d], twin)

    def near(segments):
        for s in segments:
            _, _, off, rg = spans[s]
            cov[rows_at(s, core, me, 1)] = mine[off : off + rg] * (1.0 / total)
            go(over_x(s, me))

    def middle(segments):
        for s in segments:
            over_x(s, me + 1 - 2 * xh).wait_recv()
            for d in range(1, 4):
                go(over_v(s, d, v))

    def far(segments):
        for s in segments:
            for d in range(1, 4):
                over_v(s, d, lax.rem(v + 4 - d, 4)).wait_recv()
            for d in range(1, 4):
                go(over_u(s, d, u))
            go(to_twin(s, 0, core, u))

    def relay(s):
        for d in range(1, 4):
            pu = lax.rem(u + 4 - d, 4)
            over_u(s, d, pu).wait_recv()
            go(to_twin(s, d, core, pu))

    def ready(s):
        twin_u = y + core * (z - y)
        for d in range(4):
            to_twin(s, d, 1 - core, lax.rem(twin_u + 4 - d, 4)).wait_recv()

    rows = lax.broadcasted_iota(jnp.int32, (B, B), 0)
    lanes = lax.broadcasted_iota(jnp.int32, (B, B), 1)
    bad[...] = jnp.zeros_like(bad)
    early, late = range(EARLY), range(EARLY, len(spans))
    reduce(0)
    near(early)
    middle(early)
    far(early)
    reduce(1)
    near(late)
    middle(late)
    relay(0)
    far(late)
    needs = {0: 0, 1: 1, 2: 2, 3: 3, 5: 4}

    def remainder(i, k):
        first = (starts[k] - k + i) * B
        value = cov[pl.ds(first if isinstance(i, int) else pl.multiple_of(first, B), B)]
        if k:
            ib = pl.ds(i * B if isinstance(i, int) else pl.multiple_of(i * B, B), B)
            kb, done = slice(k * B, (k + 1) * B), slice(0, k * B)
            value = value - dot3((lh[ib, done], ll[ib, done]), (lh[kb, done], ll[kb, done]), NT)
        return value

    def panel(i, k):
        ib, kb = slice(i * B, (i + 1) * B), slice(k * B, (k + 1) * B)
        lh[ib, kb], ll[ib, kb] = halves(dot3(halves(g[i]), (lh[kb, kb], ll[kb, kb]), NT))

    def pivot(k):
        kb = slice(k * B, (k + 1) * B)
        inverse_factor(g.at[k], a_scr, m_scr, bad)
        lh[kb, kb], ll[kb, kb] = halves(m_scr[...])

    def whiten(k):
        kb, done = slice(k * B, (k + 1) * B), slice(0, k * B)
        f = feat[core, k].astype(jnp.float32)
        if k:
            f = f - dot3((wh[:, done], wl[:, done]), (lh[kb, done], ll[kb, done]), NT)
        whi, wlo = halves(dot3(halves(f), (lh[kb, kb], ll[kb, kb]), NT))
        w_send[k] = whi
        if k < nb - 1:
            wh[:, kb], wl[:, kb] = whi, wlo

    ready(0)
    diagonal = jnp.where(rows == lanes, ridge, 0.0)
    g[0] = remainder(0, 0) + diagonal
    for i in range(1, nb):
        g[i] = remainder(i, 0)
    pivot(0)
    for k in range(nb):
        if k + 1 < len(spans):
            relay(k + 1)
        if k < nb - 1:
            panel(k + 1, k)
            if k + 1 in needs:
                ready(needs[k + 1])
            g[k + 1] = remainder(k + 1, k + 1) + diagonal
            pivot(k + 1)
            for i in range(k + 2, nb):
                panel(i, k)
        whiten(k)
        go(push(w_send.at[k], w_recv.at[k], w_s.at[k], w_r.at[k], blk=1 - view))

        def left(i, _):
            g[i] = remainder(i, k + 1)
            return 0

        if k < nb - 2:
            lax.fori_loop(k + 2, nb, left, 0)
    flags = push(bad, bad2, w_s.at[nb], w_r.at[nb], blk=1 - view)
    flags.start()

    half = text_ref.shape[0]
    own = pl.ds(pl.multiple_of(view * half, half), half)
    away = pl.ds(pl.multiple_of((1 - view) * half, half), half)
    for k in reversed(range(nb)):
        kb, rest = slice(k * B, (k + 1) * B), slice((k + 1) * B, nb * B)
        push(w_send.at[k], w_recv.at[k], w_s.at[k], w_r.at[k], blk=1 - view).wait_recv()
        value = w_recv[k].astype(jnp.float32)
        if k < nb - 1:
            value = value - dot3((gh[:, rest], gl[:, rest]), (lh[rest, kb], ll[rest, kb]), NN)
        value = dot3(halves(value), (lh[kb, kb], ll[kb, kb]), NN)
        if k:
            gh[:, kb], gl[:, kb] = halves(value)
        num[...] = value
        back[k] = num[away].astype(jnp.bfloat16)
        go(push(back.at[k], returned.at[k], b_s.at[k], b_r.at[k], blk=1 - view))
        text_ref[:, kb] = num[own]
        quant_ref[:, kb] = num[own]
    for k in reversed(range(nb)):
        kb = slice(k * B, (k + 1) * B)
        push(back.at[k], returned.at[k], b_s.at[k], b_r.at[k], blk=1 - view).wait_recv()
        theirs = returned[k].astype(jnp.float32)

        @pl.when(view == 0)
        def _():
            quant_ref[:, kb] = theirs

        @pl.when(view == 1)
        def _():
            text_ref[:, kb] = theirs

    flags.wait()
    flag_ref[0] = jnp.sum(bad[...] + bad2[...])
    for copy in sent:
        copy.wait_send()
    for w in range(2):
        lax.fori_loop(1, peers, lambda d, _: (scatter(w, d).wait_send(), 0)[1], 0)


def whole_step(text_emb, quant_emb, text_head, quant_head, peers, total):
    rows, emb = text_emb.shape
    n = 2 * text_head.shape[1]
    assert emb == 2 * n
    nb = n // B
    blocks = nb * (nb + 1) // 4
    chunk = blocks * B // peers
    segs = len(SEGMENTS)
    dma = pltpu.SemaphoreType.DMA
    bf = jnp.bfloat16
    f32 = jnp.float32
    return pl.pallas_call(
        functools.partial(step_kernel, total, ridge_weight),
        out_shape=[jax.ShapeDtypeStruct((rows // 2, n), f32)] * 2 + [jax.ShapeDtypeStruct((1,), f32)],
        in_specs=[HBM] * 4,
        out_specs=[VMEM] * 2 + [pl.BlockSpec(memory_space=pltpu.SMEM)],
        scratch_shapes=[
            pltpu.VMEM((2, nb, rows, B), bf),
            pltpu.VMEM((nb // 2, rows, B), bf),
            pltpu.VMEM((peers, chunk, B), bf),
            pltpu.VMEM((peers, chunk, B), bf),
            pltpu.VMEM((chunk, B), f32),
            pltpu.VMEM((2 * blocks * B, B), f32),
            pltpu.VMEM((n, n), bf),
            pltpu.VMEM((n, n), bf),
            pltpu.VMEM((nb, B, B), f32),
            pltpu.VMEM((B, B), f32),
            pltpu.VMEM((B, B), f32),
            pltpu.VMEM((rows, n), bf),
            pltpu.VMEM((rows, n), bf),
            pltpu.VMEM((nb, rows, B), bf),
            pltpu.VMEM((nb, rows, B), bf),
            pltpu.VMEM((rows, n), bf),
            pltpu.VMEM((rows, n), bf),
            pltpu.VMEM((rows, B), f32),
            pltpu.VMEM((nb, rows // 2, B), bf),
            pltpu.VMEM((nb, rows // 2, B), bf),
            pltpu.VMEM((8, B), f32),
            pltpu.VMEM((8, B), f32),
            dma((2, nb + 2)),
            dma((3, nb // 2)),
            dma((3, nb // 2)),
            dma((2, peers)),
            dma((2, peers)),
            dma((segs,)),
            dma((segs,)),
            dma((segs, 4)),
            dma((segs, 4)),
            dma((segs, 4)),
            dma((segs, 4)),
            dma((segs, 4)),
            dma((segs, 4)),
            dma((nb + 1,)),
            dma((nb + 1,)),
            dma((nb,)),
            dma((nb,)),
        ],
        compiler_params=pltpu.CompilerParams(collective_id=0, has_side_effects=True, vmem_limit_bytes=60 << 20),
    )(text_emb, quant_emb, text_head, quant_head)


def direct_kernel(c_ref, m_ref, panel):
    nb = c_ref.shape[0] // B
    rows = lax.broadcasted_iota(jnp.int32, (B, B), 0)
    cols = lax.broadcasted_iota(jnp.int32, (B, B), 1)
    lane = lax.broadcasted_iota(jnp.int32, (1, B), 1)
    sub = lax.broadcasted_iota(jnp.int32, (B, 1), 0)

    def exact(a, b, dims):
        return lax.dot_general(a, b, dims, precision=lax.Precision.HIGHEST, preferred_element_type=jnp.float32)

    def at(i):
        return pl.ds(pl.multiple_of(i * B, B), B)

    def init(i, _):
        def column(j, _):
            m_ref[at(i), at(j)] = jnp.where(j > i, 0.0, c_ref[at(i), at(j)])
            return 0

        return lax.fori_loop(0, nb, column, 0)

    lax.fori_loop(0, nb, init, 0)

    def step(k, _):
        kb = at(k)
        panel[k] = m_ref[kb, kb]

        def pivot(j, _):
            s = panel[k]
            row = panel[k, pl.ds(j, 1), :]
            p = jnp.sum(jnp.where(lane == j, row, 0.0), axis=1, keepdims=True)
            col = jnp.sum(jnp.where(cols == j, s, 0.0), axis=1, keepdims=True)
            below = sub > j
            pivot_row = jnp.where(lane == j, 1.0, row)
            left = jnp.where(jnp.logical_and(cols == j, below), 0.0, s)
            panel[k] = left - jnp.where(below, col / p, 0.0) * pivot_row
            panel[k, pl.ds(j, 1), :] = jnp.where(lane <= j, pivot_row, 0.0) * lax.rsqrt(p)
            return 0

        lax.fori_loop(0, B, pivot, 0)
        m_ref[kb, kb] = panel[k]

        def inverse_row(j, _):
            m_ref[kb, at(j)] = exact(m_ref[kb, kb], m_ref[kb, at(j)], NN)
            return 0

        lax.fori_loop(0, k, inverse_row, 0)

        def factor(i, _):
            panel[i] = exact(m_ref[at(i), kb], m_ref[kb, kb], NT)
            m_ref[at(i), kb] = jnp.zeros((B, B), jnp.float32)
            return 0

        lax.fori_loop(k + 1, nb, factor, 0)

        def update(i, _):
            def inverse_part(j, _):
                m_ref[at(i), at(j)] = m_ref[at(i), at(j)] - exact(panel[i], m_ref[kb, at(j)], NN)
                return 0

            lax.fori_loop(0, k + 1, inverse_part, 0)

            def schur(j, _):
                m_ref[at(i), at(j)] = m_ref[at(i), at(j)] - exact(panel[i], panel[j], NT)
                return 0

            return lax.fori_loop(k + 1, i + 1, schur, 0)

        return lax.fori_loop(k + 1, nb, update, 0)

    lax.fori_loop(0, nb, step, 0)


def direct_step(text_emb, quant_emb, text_head, quant_head, total):
    view = lax.axis_index("blk")
    ranks = lax.axis_size("rows")
    h = jnp.stack(
        [
            jnp.dot(text_emb, text_head, preferred_element_type=jnp.float32).astype(jnp.bfloat16),
            jnp.dot(quant_emb, quant_head, preferred_element_type=jnp.float32).astype(jnp.bfloat16),
        ]
    )

    def swapped(x):
        return lax.ppermute(x, "blk", [(0, 1), (1, 0)])

    near = lax.dynamic_index_in_dim(h, view, 0, keepdims=False)
    far = swapped(lax.dynamic_index_in_dim(h, 1 - view, 0, keepdims=False))
    feat = jnp.where(view == 0, jnp.concatenate([near, far], 1), jnp.concatenate([far, near], 1))
    n = feat.shape[1]
    cov = mm(feat, feat, TN)
    hop = 1
    while hop < ranks:
        cov = cov + lax.ppermute(cov, "rows", [(r, r ^ hop) for r in range(ranks)])
        hop *= 2
    cov = cov / total + ridge_weight * jnp.eye(n, dtype=jnp.float32)
    inverse = pl.pallas_call(
        direct_kernel,
        out_shape=jax.ShapeDtypeStruct((n, n), jnp.float32),
        in_specs=[VMEM],
        out_specs=VMEM,
        scratch_shapes=[pltpu.VMEM((n // B, B, B), jnp.float32)],
        compiler_params=pltpu.CompilerParams(vmem_limit_bytes=56 << 20),
    )(cov)
    exact = functools.partial(
        lax.dot_general, precision=lax.Precision.HIGHEST, preferred_element_type=jnp.float32
    )
    white = swapped(exact(feat.astype(jnp.float32), inverse, NT))
    grad = exact(white, inverse, NN)
    half = grad.shape[0] // 2
    own = lax.dynamic_slice_in_dim(grad, view * half, half, 0)
    other = swapped(lax.dynamic_slice_in_dim(grad, (1 - view) * half, half, 0))
    return jnp.where(view == 0, own, other), jnp.where(view == 0, other, own)


def shards(*arrays):
    peers = lax.axis_size("rows") // 2
    total = arrays[0].shape[0] * lax.axis_size("rows")
    text, quant, flag = whole_step(*arrays, peers, total)
    return lax.cond(flag[0] > 0, lambda: direct_step(*arrays, total), lambda: (text, quant))


def solution(mesh):
    placed = (P("rows", None), P("rows", None), P(None, "blk"), P(None, "blk"))
    return jax.shard_map(
        shards,
        mesh=mesh,
        in_specs=placed,
        out_specs=(P(("rows", "blk"), None), P(("rows", "blk"), None)),
        check_vma=False,
    )
```

```python
import functools

import jax
import jax.numpy as jnp
from jax import lax
from jax.experimental import pallas as pl
from jax.experimental.pallas import tpu as pltpu
from jax.sharding import PartitionSpec as P

ridge_weight = 0.05
B = 256
NN = (((1,), (0,)), ((), ()))
NT = (((1,), (1,)), ((), ()))
TN = (((0,), (0,)), ((), ()))
MESH = pl.DeviceIdType.MESH
VMEM = pl.BlockSpec(memory_space=pltpu.VMEM)
HBM = pl.BlockSpec(memory_space=pl.ANY)


def mm(a, b, dims):
    return lax.dot_general(a, b, dims, preferred_element_type=jnp.float32)


def halves(x):
    hi = x.astype(jnp.bfloat16)
    return hi, (x - hi.astype(jnp.float32)).astype(jnp.bfloat16)


def dot3(a, b, dims):
    (ah, al), (bh, bl) = a, b
    return mm(ah, bh, dims) + (mm(ah, bl, dims) + mm(al, bh, dims))


def push(src, dst, send, recv, **device):
    return pltpu.make_async_remote_copy(
        src_ref=src, dst_ref=dst, send_sem=send, recv_sem=recv, device_id=device, device_id_type=MESH
    )

SEGMENTS = ((0, 4), (8, 4), (16, 4), (24, 4), (32, 2))
EARLY = 2


def inverse_factor(s_ref, m_ref, bad_ref):
    rows = lax.broadcasted_iota(jnp.int32, (B, B), 0)
    cols = lax.broadcasted_iota(jnp.int32, (B, B), 1)
    eye = jnp.where(rows == cols, 1.0, 0.0)
    weight = jnp.where(rows > cols, 1.0, jnp.where(rows == cols, 0.5, 0.0))
    s = s_ref[...]
    on = jnp.where(rows == cols, s, 0.0)
    sc = lax.rsqrt(jnp.sum(on, axis=1, keepdims=True))
    sr = lax.rsqrt(jnp.sum(on, axis=0, keepdims=True))
    a = jnp.where(rows == cols, 1.0, s * sc * sr)
    step = eye - weight * (a - eye)
    m_ref[...] = step * sr
    bf = jnp.bfloat16
    t = (eye - weight * (a - eye)).astype(bf)
    a = mm(mm(t, a.astype(bf), NN).astype(bf), t, NT)
    t = (eye - weight * (a - eye)).astype(bf)
    m_ref[...] = mm(t, m_ref[...].astype(bf), NN)
    a = mm(mm(t, a.astype(bf), NN).astype(bf), t, NT)
    t = (eye - weight * (a - eye)).astype(bf)
    m_ref[...] = mm(t, m_ref[...].astype(bf), NN)
    t = halves(m_ref[...])
    gap = dot3(halves(dot3(t, halves(s_ref[...]), NN)), t, NT) - eye
    far_off = jnp.sum(jnp.sum(gap * gap, axis=0, keepdims=True), axis=1, keepdims=True)
    bad_ref[...] += jnp.where(far_off <= 0.06, 0.0, 1.0)
    m_ref[...] = dot3(halves(eye - weight * gap), halves(m_ref[...]), NN)


def step_kernel(
    total, ridge, text_emb, quant_emb, text_head, quant_head, text_ref, quant_ref, flag_ref,
    feat, away_feat, part, arrived, mine, cov, lh, ll, g, m_scr, wh, wl, w_send, w_recv, gh, gl, num, back, returned, bad, bad2,
    h_sem, e_send, e_recv, s_send, s_recv, x_send, x_recv, v_send, v_recv, u_send, u_recv, t_send, t_recv, w_s, w_r, b_s, b_r,
):
    at = lax.axis_index("rows")
    view = lax.axis_index("blk")
    core, xh, y, z = lax.rem(at, 2), lax.rem(at // 2, 2), lax.rem(at // 4, 4), at // 16
    twin = at + 1 - 2 * core
    peers = arrived.shape[0]
    nb = lh.shape[0] // B
    per = nb // 2
    starts = [sum(nb - c for c in range(k)) for k in range(nb)]
    order = [(i, j) for j in range(nb) for i in range(j, nb)]
    u, v = z + core * (y - z), y + core * (z - y)

    def device(p_u, p_v, p_x):
        pz, py = p_u + core * (p_v - p_u), p_v + core * (p_u - p_v)
        return ((pz * 4 + py) * 2 + p_x) * 2 + core

    def device_of(p):
        return device(p // 8, lax.rem(p // 2, 4), lax.rem(p, 2))

    me = (u * 4 + v) * 2 + xh

    depth = text_emb.shape[1] // 2
    places = ((wh, wl, lh), (gh, gl, ll))

    def for_view(which, text, quant):
        @pl.when(view == 1 - which)
        def _():
            text()

        @pl.when(view == which)
        def _():
            quant()

    def emb_copy(src, which, half):
        part_of = src.at[:, half * depth : (half + 1) * depth]
        return pltpu.make_async_copy(part_of, places[which][half], h_sem.at[which, 2 * per + half])

    def head_copy(src, which, half, c):
        part_of = src.at[half * depth : (half + 1) * depth, c * B : (c + 1) * B]
        at_cols = slice((half * per + c) * B, (half * per + c + 1) * B)
        return pltpu.make_async_copy(part_of, places[which][2].at[:, at_cols], h_sem.at[which, 2 * c + half])

    def fetch(which, emb, head):
        for half in range(2):
            emb_copy(emb, which, half).start()
        for c in range(per):
            for half in range(2):
                head_copy(head, which, half, c).start()

    for which in range(2):
        for_view(which, lambda: fetch(which, text_emb, text_head), lambda: fetch(which, quant_emb, quant_head))

    barrier = pltpu.get_barrier_semaphore()

    def greet(d, _):
        pl.semaphore_signal(barrier, inc=1, device_id={"rows": device_of(lax.rem(me + d, peers))}, device_id_type=MESH)
        return 0

    pl.semaphore_signal(barrier, inc=1, device_id={"blk": 1 - view}, device_id_type=MESH)
    pl.semaphore_signal(barrier, inc=1, device_id={"rows": twin}, device_id_type=MESH)
    lax.fori_loop(1, peers, greet, 0)

    def project(which, c):
        emb0, emb1, head = places[which]
        for half in range(2):
            head_copy(text_head, which, half, c).wait()
        lo, hi = slice(c * B, (c + 1) * B), slice((per + c) * B, (per + c + 1) * B)
        return (mm(emb0[...], head[:, lo], NN) + mm(emb1[...], head[:, hi], NN)).astype(jnp.bfloat16)

    sent = []

    def go(copy):
        copy.start()
        sent.append(copy)

    def swap(c, which_view):
        return push(away_feat.at[c], feat.at[core, which_view * per + c], e_send.at[0, c], e_recv.at[0, c], blk=1 - view)

    def share(turn, which_core, b):
        c = lax.rem(b, per)
        block = feat.at[which_core, b]
        return push(block, block, e_send.at[turn, c], e_recv.at[turn, c], rows=twin)

    for which in range(2):
        for half in range(2):
            emb_copy(text_emb, which, half).wait()
        for c in range(per):
            if which == 0:
                away_feat[c] = project(which, c)
                if c == 0:
                    pl.semaphore_wait(barrier, peers + 1)
                go(swap(c, view))
            else:
                feat[core, view * per + c] = project(which, c)
                go(share(1, core, view * per + c))
    for c in range(per):
        swap(c, 1 - view).wait_recv()
        go(share(2, core, (1 - view) * per + c))
    for c in range(per):
        share(1, 1 - core, view * per + c).wait_recv()
    for c in range(per):
        share(2, 1 - core, (1 - view) * per + c).wait_recv()

    offset = 0
    spans = []
    for begin, count in SEGMENTS:
        rg = count * B // peers
        spans.append((begin, count, offset, rg))
        for t in range(count):
            (i0, j0), (i1, j1) = order[begin + t], order[begin + count + t]
            i, j = i0 + core * (i1 - i0), j0 + core * (j1 - j0)
            block = mm(feat[0, i], feat[0, j], TN) + mm(feat[1, i], feat[1, j], TN)
            n = B // rg
            part[t * n : (t + 1) * n, offset : offset + rg] = block.astype(jnp.bfloat16).reshape(n, rg, B)
        offset += rg

    cut = spans[EARLY][2]
    waves = [(0, cut), (cut, mine.shape[0] - cut)]

    def scatter(w, d):
        p = lax.rem(me + d, peers)
        piece = pl.ds(*waves[w])
        return push(part.at[p, piece], arrived.at[me, piece], s_send.at[w, d], s_recv.at[w, d], rows=device_of(p))

    def landed(w, d):
        p = lax.rem(me + peers - d, peers)
        piece = pl.ds(*waves[w])
        return push(part.at[p, piece], arrived.at[p, piece], s_send.at[w, d], s_recv.at[w, d], rows=device_of(p))

    for w in range(2):
        lax.fori_loop(1, peers, lambda d, _: (scatter(w, d).start(), 0)[1], 0)

    def reduce(w):
        piece = pl.ds(*waves[w])
        mine[piece] = part[me, piece].astype(jnp.float32)

        def add(d, _):
            landed(w, d).wait_recv()
            mine[piece] += arrived[lax.rem(me + peers - d, peers), piece].astype(jnp.float32)
            return 0

        lax.fori_loop(1, peers, add, 0)

    def rows_at(s, c, piece, count):
        begin, size, _, rg = spans[s]
        return pl.ds(pl.multiple_of((begin + c * size) * B + piece * rg, 16), count * rg)

    def same(rows, send, recv, dev):
        return push(cov.at[rows], cov.at[rows], send, recv, rows=dev)

    def over_x(s, piece):
        return same(rows_at(s, core, piece, 1), x_send.at[s], x_recv.at[s], device(u, v, 1 - xh))

    def over_v(s, d, pv):
        return same(rows_at(s, core, (u * 4 + pv) * 2, 2), v_send.at[s, d], v_recv.at[s, d], device(u, lax.rem(v + d, 4), xh))

    def over_u(s, d, pu):
        return same(rows_at(s, core, pu * 8, 8), u_send.at[s, d], u_recv.at[s, d], device(lax.rem(u + d, 4), v, xh))

    def to_twin(s, d, c, pu):
        return same(rows_at(s, c, pu * 8, 8), t_send.at[s, d], t_recv.at[s, d], twin)

    def near(segments):
        for s in segments:
            _, _, off, rg = spans[s]
            cov[rows_at(s, core, me, 1)] = mine[off : off + rg] * (1.0 / total)
            go(over_x(s, me))

    def middle(segments):
        for s in segments:
            over_x(s, me + 1 - 2 * xh).wait_recv()
            for d in range(1, 4):
                go(over_v(s, d, v))

    def far(segments):
        for s in segments:
            for d in range(1, 4):
                over_v(s, d, lax.rem(v + 4 - d, 4)).wait_recv()
            for d in range(1, 4):
                go(over_u(s, d, u))
            go(to_twin(s, 0, core, u))

    def relay(s):
        for d in range(1, 4):
            pu = lax.rem(u + 4 - d, 4)
            over_u(s, d, pu).wait_recv()
            go(to_twin(s, d, core, pu))

    def ready(s):
        twin_u = y + core * (z - y)
        for d in range(4):
            to_twin(s, d, 1 - core, lax.rem(twin_u + 4 - d, 4)).wait_recv()

    rows = lax.broadcasted_iota(jnp.int32, (B, B), 0)
    lanes = lax.broadcasted_iota(jnp.int32, (B, B), 1)
    bad[...] = jnp.zeros_like(bad)
    early, late = range(EARLY), range(EARLY, len(spans))
    reduce(0)
    near(early)
    middle(early)
    far(early)
    reduce(1)
    near(late)
    middle(late)
    relay(0)
    far(late)
    needs = {0: 0, 1: 1, 2: 2, 3: 3, 5: 4}

    def remainder(i, k):
        first = (starts[k] - k + i) * B
        value = cov[pl.ds(first if isinstance(i, int) else pl.multiple_of(first, B), B)]
        if k:
            ib = pl.ds(i * B if isinstance(i, int) else pl.multiple_of(i * B, B), B)
            kb, done = slice(k * B, (k + 1) * B), slice(0, k * B)
            value = value - dot3((lh[ib, done], ll[ib, done]), (lh[kb, done], ll[kb, done]), NT)
        return value

    def panel(i, k):
        ib, kb = slice(i * B, (i + 1) * B), slice(k * B, (k + 1) * B)
        lh[ib, kb], ll[ib, kb] = halves(dot3(halves(g[i]), (lh[kb, kb], ll[kb, kb]), NT))

    def pivot(k):
        kb = slice(k * B, (k + 1) * B)
        inverse_factor(g.at[k], m_scr, bad)
        lh[kb, kb], ll[kb, kb] = halves(m_scr[...])

    def whiten(k):
        kb, done = slice(k * B, (k + 1) * B), slice(0, k * B)
        f = feat[core, k].astype(jnp.float32)
        if k:
            f = f - dot3((wh[:, done], wl[:, done]), (lh[kb, done], ll[kb, done]), NT)
        whi, wlo = halves(dot3(halves(f), (lh[kb, kb], ll[kb, kb]), NT))
        w_send[k] = whi
        if k < nb - 1:
            wh[:, kb], wl[:, kb] = whi, wlo

    ready(0)
    diagonal = jnp.where(rows == lanes, ridge, 0.0)
    g[0] = remainder(0, 0) + diagonal
    for i in range(1, nb):
        g[i] = remainder(i, 0)
    pivot(0)
    for k in range(nb):
        if k + 1 < len(spans):
            relay(k + 1)
        if k < nb - 1:
            panel(k + 1, k)
            if k + 1 in needs:
                ready(needs[k + 1])
            g[k + 1] = remainder(k + 1, k + 1) + diagonal
            pivot(k + 1)
            for i in range(k + 2, nb):
                panel(i, k)
        for i in range(k + 2, nb):
            g[i] = remainder(i, k + 1)
        whiten(k)
        go(push(w_send.at[k], w_recv.at[k], w_s.at[k], w_r.at[k], blk=1 - view))
    flags = push(bad, bad2, w_s.at[nb], w_r.at[nb], blk=1 - view)
    flags.start()

    half = text_ref.shape[0]
    own = pl.ds(pl.multiple_of(view * half, half), half)
    away = pl.ds(pl.multiple_of((1 - view) * half, half), half)
    for k in reversed(range(nb)):
        kb, rest = slice(k * B, (k + 1) * B), slice((k + 1) * B, nb * B)
        push(w_send.at[k], w_recv.at[k], w_s.at[k], w_r.at[k], blk=1 - view).wait_recv()
        value = w_recv[k].astype(jnp.float32)
        if k < nb - 1:
            value = value - dot3((gh[:, rest], gl[:, rest]), (lh[rest, kb], ll[rest, kb]), NN)
        value = dot3(halves(value), (lh[kb, kb], ll[kb, kb]), NN)
        if k:
            gh[:, kb], gl[:, kb] = halves(value)
        num[...] = value
        back[k] = num[away].astype(jnp.bfloat16)
        go(push(back.at[k], returned.at[k], b_s.at[k], b_r.at[k], blk=1 - view))
        text_ref[:, kb] = num[own]
        quant_ref[:, kb] = num[own]
    for k in reversed(range(nb)):
        kb = slice(k * B, (k + 1) * B)
        push(back.at[k], returned.at[k], b_s.at[k], b_r.at[k], blk=1 - view).wait_recv()
        theirs = returned[k].astype(jnp.float32)

        @pl.when(view == 0)
        def _():
            quant_ref[:, kb] = theirs

        @pl.when(view == 1)
        def _():
            text_ref[:, kb] = theirs

    flags.wait()
    flag_ref[0] = jnp.sum(bad[...] + bad2[...])
    for copy in sent:
        copy.wait_send()
    for w in range(2):
        lax.fori_loop(1, peers, lambda d, _: (scatter(w, d).wait_send(), 0)[1], 0)


def whole_step(text_emb, quant_emb, text_head, quant_head, peers, total):
    rows, emb = text_emb.shape
    n = 2 * text_head.shape[1]
    assert emb == 2 * n
    nb = n // B
    blocks = nb * (nb + 1) // 4
    chunk = blocks * B // peers
    segs = len(SEGMENTS)
    dma = pltpu.SemaphoreType.DMA
    bf = jnp.bfloat16
    f32 = jnp.float32
    return pl.pallas_call(
        functools.partial(step_kernel, total, ridge_weight),
        out_shape=[jax.ShapeDtypeStruct((rows // 2, n), f32)] * 2 + [jax.ShapeDtypeStruct((1,), f32)],
        in_specs=[HBM] * 4,
        out_specs=[VMEM] * 2 + [pl.BlockSpec(memory_space=pltpu.SMEM)],
        scratch_shapes=[
            pltpu.VMEM((2, nb, rows, B), bf),
            pltpu.VMEM((nb // 2, rows, B), bf),
            pltpu.VMEM((peers, chunk, B), bf),
            pltpu.VMEM((peers, chunk, B), bf),
            pltpu.VMEM((chunk, B), f32),
            pltpu.VMEM((2 * blocks * B, B), f32),
            pltpu.VMEM((n, n), bf),
            pltpu.VMEM((n, n), bf),
            pltpu.VMEM((nb, B, B), f32),
            pltpu.VMEM((B, B), f32),
            pltpu.VMEM((rows, n), bf),
            pltpu.VMEM((rows, n), bf),
            pltpu.VMEM((nb, rows, B), bf),
            pltpu.VMEM((nb, rows, B), bf),
            pltpu.VMEM((rows, n), bf),
            pltpu.VMEM((rows, n), bf),
            pltpu.VMEM((rows, B), f32),
            pltpu.VMEM((nb, rows // 2, B), bf),
            pltpu.VMEM((nb, rows // 2, B), bf),
            pltpu.VMEM((8, B), f32),
            pltpu.VMEM((8, B), f32),
            dma((2, nb + 2)),
            dma((3, nb // 2)),
            dma((3, nb // 2)),
            dma((2, peers)),
            dma((2, peers)),
            dma((segs,)),
            dma((segs,)),
            dma((segs, 4)),
            dma((segs, 4)),
            dma((segs, 4)),
            dma((segs, 4)),
            dma((segs, 4)),
            dma((segs, 4)),
            dma((nb + 1,)),
            dma((nb + 1,)),
            dma((nb,)),
            dma((nb,)),
        ],
        compiler_params=pltpu.CompilerParams(collective_id=0, has_side_effects=True, vmem_limit_bytes=60 << 20),
    )(text_emb, quant_emb, text_head, quant_head)


def direct_kernel(c_ref, m_ref, panel):
    nb = c_ref.shape[0] // B
    rows = lax.broadcasted_iota(jnp.int32, (B, B), 0)
    cols = lax.broadcasted_iota(jnp.int32, (B, B), 1)
    lane = lax.broadcasted_iota(jnp.int32, (1, B), 1)
    sub = lax.broadcasted_iota(jnp.int32, (B, 1), 0)

    def exact(a, b, dims):
        return lax.dot_general(a, b, dims, precision=lax.Precision.HIGHEST, preferred_element_type=jnp.float32)

    def at(i):
        return pl.ds(pl.multiple_of(i * B, B), B)

    def init(i, _):
        def column(j, _):
            m_ref[at(i), at(j)] = jnp.where(j > i, 0.0, c_ref[at(i), at(j)])
            return 0

        return lax.fori_loop(0, nb, column, 0)

    lax.fori_loop(0, nb, init, 0)

    def step(k, _):
        kb = at(k)
        panel[k] = m_ref[kb, kb]

        def pivot(j, _):
            s = panel[k]
            row = panel[k, pl.ds(j, 1), :]
            p = jnp.sum(jnp.where(lane == j, row, 0.0), axis=1, keepdims=True)
            col = jnp.sum(jnp.where(cols == j, s, 0.0), axis=1, keepdims=True)
            below = sub > j
            pivot_row = jnp.where(lane == j, 1.0, row)
            left = jnp.where(jnp.logical_and(cols == j, below), 0.0, s)
            panel[k] = left - jnp.where(below, col / p, 0.0) * pivot_row
            panel[k, pl.ds(j, 1), :] = jnp.where(lane <= j, pivot_row, 0.0) * lax.rsqrt(p)
            return 0

        lax.fori_loop(0, B, pivot, 0)
        m_ref[kb, kb] = panel[k]

        def inverse_row(j, _):
            m_ref[kb, at(j)] = exact(m_ref[kb, kb], m_ref[kb, at(j)], NN)
            return 0

        lax.fori_loop(0, k, inverse_row, 0)

        def factor(i, _):
            panel[i] = exact(m_ref[at(i), kb], m_ref[kb, kb], NT)
            m_ref[at(i), kb] = jnp.zeros((B, B), jnp.float32)
            return 0

        lax.fori_loop(k + 1, nb, factor, 0)

        def update(i, _):
            def inverse_part(j, _):
                m_ref[at(i), at(j)] = m_ref[at(i), at(j)] - exact(panel[i], m_ref[kb, at(j)], NN)
                return 0

            lax.fori_loop(0, k + 1, inverse_part, 0)

            def schur(j, _):
                m_ref[at(i), at(j)] = m_ref[at(i), at(j)] - exact(panel[i], panel[j], NT)
                return 0

            return lax.fori_loop(k + 1, i + 1, schur, 0)

        return lax.fori_loop(k + 1, nb, update, 0)

    lax.fori_loop(0, nb, step, 0)


def direct_step(text_emb, quant_emb, text_head, quant_head, total):
    view = lax.axis_index("blk")
    ranks = lax.axis_size("rows")
    h = jnp.stack(
        [
            jnp.dot(text_emb, text_head, preferred_element_type=jnp.float32).astype(jnp.bfloat16),
            jnp.dot(quant_emb, quant_head, preferred_element_type=jnp.float32).astype(jnp.bfloat16),
        ]
    )

    def swapped(x):
        return lax.ppermute(x, "blk", [(0, 1), (1, 0)])

    near = lax.dynamic_index_in_dim(h, view, 0, keepdims=False)
    far = swapped(lax.dynamic_index_in_dim(h, 1 - view, 0, keepdims=False))
    feat = jnp.where(view == 0, jnp.concatenate([near, far], 1), jnp.concatenate([far, near], 1))
    n = feat.shape[1]
    cov = mm(feat, feat, TN)
    hop = 1
    while hop < ranks:
        cov = cov + lax.ppermute(cov, "rows", [(r, r ^ hop) for r in range(ranks)])
        hop *= 2
    cov = cov / total + ridge_weight * jnp.eye(n, dtype=jnp.float32)
    inverse = pl.pallas_call(
        direct_kernel,
        out_shape=jax.ShapeDtypeStruct((n, n), jnp.float32),
        in_specs=[VMEM],
        out_specs=VMEM,
        scratch_shapes=[pltpu.VMEM((n // B, B, B), jnp.float32)],
        compiler_params=pltpu.CompilerParams(vmem_limit_bytes=56 << 20),
    )(cov)
    exact = functools.partial(
        lax.dot_general, precision=lax.Precision.HIGHEST, preferred_element_type=jnp.float32
    )
    white = swapped(exact(feat.astype(jnp.float32), inverse, NT))
    grad = exact(white, inverse, NN)
    half = grad.shape[0] // 2
    own = lax.dynamic_slice_in_dim(grad, view * half, half, 0)
    other = swapped(lax.dynamic_slice_in_dim(grad, (1 - view) * half, half, 0))
    return jnp.where(view == 0, own, other), jnp.where(view == 0, other, own)


def shards(*arrays):
    peers = lax.axis_size("rows") // 2
    total = arrays[0].shape[0] * lax.axis_size("rows")
    text, quant, flag = whole_step(*arrays, peers, total)
    return lax.cond(flag[0] > 0, lambda: direct_step(*arrays, total), lambda: (text + flag[0], quant + flag[0]))


def solution(mesh):
    placed = (P("rows", None), P("rows", None), P(None, "blk"), P(None, "blk"))
    return jax.shard_map(
        shards,
        mesh=mesh,
        in_specs=placed,
        out_specs=(P(("rows", "blk"), None), P(("rows", "blk"), None)),
        check_vma=False,
    )
```

```python
import functools

import jax
import jax.numpy as jnp
from jax import lax
from jax.experimental import pallas as pl
from jax.experimental.pallas import tpu as pltpu
from jax.sharding import PartitionSpec as P

ridge_weight = 0.05
B = 256
NN = (((1,), (0,)), ((), ()))
NT = (((1,), (1,)), ((), ()))
TN = (((0,), (0,)), ((), ()))
MESH = pl.DeviceIdType.MESH
VMEM = pl.BlockSpec(memory_space=pltpu.VMEM)
HBM = pl.BlockSpec(memory_space=pl.ANY)


def mm(a, b, dims):
    return lax.dot_general(a, b, dims, preferred_element_type=jnp.float32)


def halves(x):
    hi = x.astype(jnp.bfloat16)
    return hi, (x - hi.astype(jnp.float32)).astype(jnp.bfloat16)


def dot3(a, b, dims):
    (ah, al), (bh, bl) = a, b
    return mm(ah, bh, dims) + (mm(ah, bl, dims) + mm(al, bh, dims))


def push(src, dst, send, recv, **device):
    return pltpu.make_async_remote_copy(
        src_ref=src, dst_ref=dst, send_sem=send, recv_sem=recv, device_id=device, device_id_type=MESH
    )

SEGMENTS = ((0, 4), (8, 4), (16, 4), (24, 4), (32, 2))
EARLY = 2


def inverse_factor(s_ref, m_ref, bad_ref):
    rows = lax.broadcasted_iota(jnp.int32, (B, B), 0)
    cols = lax.broadcasted_iota(jnp.int32, (B, B), 1)
    eye = jnp.where(rows == cols, 1.0, 0.0)
    weight = jnp.where(rows > cols, 1.0, jnp.where(rows == cols, 0.5, 0.0))
    s = s_ref[...]
    on = jnp.where(rows == cols, s, 0.0)
    sc = lax.rsqrt(jnp.sum(on, axis=1, keepdims=True))
    sr = lax.rsqrt(jnp.sum(on, axis=0, keepdims=True))
    a = jnp.where(rows == cols, 1.0, s * sc * sr)
    step = eye - weight * (a - eye)
    m_ref[...] = step * sr
    bf = jnp.bfloat16
    t = (eye - weight * (a - eye)).astype(bf)
    a = mm(mm(t, a.astype(bf), NN).astype(bf), t, NT)
    t = (eye - weight * (a - eye)).astype(bf)
    m_ref[...] = mm(t, m_ref[...].astype(bf), NN)
    a = mm(mm(t, a.astype(bf), NN).astype(bf), t, NT)
    t = (eye - weight * (a - eye)).astype(bf)
    m_ref[...] = mm(t, m_ref[...].astype(bf), NN)
    t = halves(m_ref[...])
    gap = dot3(halves(dot3(t, halves(s_ref[...]), NN)), t, NT) - eye
    far_off = jnp.sum(jnp.sum(gap * gap, axis=0, keepdims=True), axis=1, keepdims=True)
    bad_ref[...] += jnp.where(far_off <= 0.06, 0.0, 1.0)
    m_ref[...] = dot3(halves(eye - weight * gap), halves(m_ref[...]), NN)


def step_kernel(
    total, ridge, text_emb, quant_emb, text_head, quant_head, text_ref, quant_ref, flag_ref,
    feat, away_feat, part, arrived, mine, cov, lh, ll, g, m_scr, wh, wl, w_send, w_recv, gh, gl, num, back, returned, bad, bad2,
    h_sem, e_send, e_recv, s_send, s_recv, v_send, v_recv, u_send, u_recv, t_send, t_recv, w_s, w_r, b_s, b_r,
):
    at = lax.axis_index("rows")
    view = lax.axis_index("blk")
    core, xh, y, z = lax.rem(at, 2), lax.rem(at // 2, 2), lax.rem(at // 4, 4), at // 16
    twin = at + 1 - 2 * core
    peers = arrived.shape[0]
    nb = lh.shape[0] // B
    per = nb // 2
    starts = [sum(nb - c for c in range(k)) for k in range(nb)]
    order = [(i, j) for j in range(nb) for i in range(j, nb)]
    u, v = z + core * (y - z), y + core * (z - y)

    def device(p_u, p_v, p_x):
        pz, py = p_u + core * (p_v - p_u), p_v + core * (p_u - p_v)
        return ((pz * 4 + py) * 2 + p_x) * 2 + core

    def device_of(p):
        return device(p // 8, lax.rem(p // 2, 4), lax.rem(p, 2))

    me = (u * 4 + v) * 2 + xh

    depth = text_emb.shape[1] // 2
    places = ((wh, wl, lh), (gh, gl, ll))

    def for_view(which, text, quant):
        @pl.when(view == 1 - which)
        def _():
            text()

        @pl.when(view == which)
        def _():
            quant()

    def emb_copy(src, which, half):
        part_of = src.at[:, half * depth : (half + 1) * depth]
        return pltpu.make_async_copy(part_of, places[which][half], h_sem.at[which, 2 * per + half])

    def head_copy(src, which, half, c):
        part_of = src.at[half * depth : (half + 1) * depth, c * B : (c + 1) * B]
        at_cols = slice((half * per + c) * B, (half * per + c + 1) * B)
        return pltpu.make_async_copy(part_of, places[which][2].at[:, at_cols], h_sem.at[which, 2 * c + half])

    def fetch(turn):
        which, c = turn // per, turn % per

        def start(emb, head):
            for half in range(2):
                if c == 0:
                    emb_copy(emb, which, half).start()
                head_copy(head, which, half, c).start()

        for_view(which, lambda: start(text_emb, text_head), lambda: start(quant_emb, quant_head))

    for turn in range(2):
        fetch(turn)

    barrier = pltpu.get_barrier_semaphore()

    def greet(d, _):
        pl.semaphore_signal(barrier, inc=1, device_id={"rows": device_of(lax.rem(me + d, peers))}, device_id_type=MESH)
        return 0

    pl.semaphore_signal(barrier, inc=1, device_id={"blk": 1 - view}, device_id_type=MESH)
    pl.semaphore_signal(barrier, inc=1, device_id={"rows": twin}, device_id_type=MESH)
    lax.fori_loop(1, peers, greet, 0)

    def project(which, c):
        emb0, emb1, head = places[which]
        for half in range(2):
            head_copy(text_head, which, half, c).wait()
        lo, hi = slice(c * B, (c + 1) * B), slice((per + c) * B, (per + c + 1) * B)
        return (mm(emb0[...], head[:, lo], NN) + mm(emb1[...], head[:, hi], NN)).astype(jnp.bfloat16)

    sent = []

    def go(copy):
        copy.start()
        sent.append(copy)

    def swap(c, which_view):
        return push(away_feat.at[c], feat.at[core, which_view * per + c], e_send.at[0, c], e_recv.at[0, c], blk=1 - view)

    def share(turn, which_core, b):
        c = lax.rem(b, per)
        block = feat.at[which_core, b]
        return push(block, block, e_send.at[turn, c], e_recv.at[turn, c], rows=twin)

    for which in range(2):
        for half in range(2):
            emb_copy(text_emb, which, half).wait()
        for c in range(per):
            if which * per + c + 2 < 2 * per:
                fetch(which * per + c + 2)
            if which == 0:
                away_feat[c] = project(which, c)
                if c == 0:
                    pl.semaphore_wait(barrier, peers + 1)
                go(swap(c, view))
            else:
                feat[core, view * per + c] = project(which, c)
                go(share(1, core, view * per + c))
    for c in range(per):
        swap(c, 1 - view).wait_recv()
        go(share(2, core, (1 - view) * per + c))
    for c in range(per):
        share(1, 1 - core, view * per + c).wait_recv()
    for c in range(per):
        share(2, 1 - core, (1 - view) * per + c).wait_recv()

    offset = 0
    spans = []
    for begin, count in SEGMENTS:
        rg = count * B // peers
        spans.append((begin, count, offset, rg))
        offset += rg

    def products(segments):
        for begin, count, off, rg in segments:
            for t in range(count):
                (i0, j0), (i1, j1) = order[begin + t], order[begin + count + t]
                i, j = i0 + core * (i1 - i0), j0 + core * (j1 - j0)
                block = mm(feat[0, i], feat[0, j], TN) + mm(feat[1, i], feat[1, j], TN)
                n = B // rg
                part[t * n : (t + 1) * n, off : off + rg] = block.astype(jnp.bfloat16).reshape(n, rg, B)

    cut = spans[EARLY][2]
    waves = [(0, cut), (cut, mine.shape[0] - cut)]

    def scatter(w, d):
        p = lax.rem(me + d, peers)
        piece = pl.ds(*waves[w])
        return push(part.at[p, piece], arrived.at[me, piece], s_send.at[w, d], s_recv.at[w, d], rows=device_of(p))

    def landed(w, d):
        p = lax.rem(me + peers - d, peers)
        piece = pl.ds(*waves[w])
        return push(part.at[p, piece], arrived.at[p, piece], s_send.at[w, d], s_recv.at[w, d], rows=device_of(p))

    for w, segments in enumerate((spans[:EARLY], spans[EARLY:])):
        products(segments)
        lax.fori_loop(1, peers, lambda d, _: (scatter(w, d).start(), 0)[1], 0)

    def reduce(w):
        piece = pl.ds(*waves[w])
        mine[piece] = part[me, piece].astype(jnp.float32)

        def add(d, _):
            landed(w, d).wait_recv()
            mine[piece] += arrived[lax.rem(me + peers - d, peers), piece].astype(jnp.float32)
            return 0

        lax.fori_loop(1, peers, add, 0)

    def rows_at(s, c, piece, count):
        begin, size, _, rg = spans[s]
        return pl.ds(pl.multiple_of((begin + c * size) * B + piece * rg, 16), count * rg)

    def same(rows, send, recv, dev):
        return push(cov.at[rows], cov.at[rows], send, recv, rows=dev)

    def close_by(s, d, piece):
        there = device(u, lax.rem(v + d // 2, 4), lax.rem(xh + d, 2))
        return same(rows_at(s, core, piece, 1), v_send.at[s, d], v_recv.at[s, d], there)

    def over_u(s, d, pu):
        return same(rows_at(s, core, pu * 8, 8), u_send.at[s, d], u_recv.at[s, d], device(lax.rem(u + d, 4), v, xh))

    def to_twin(s, d, c, pu):
        return same(rows_at(s, c, pu * 8, 8), t_send.at[s, d], t_recv.at[s, d], twin)

    def near(segments):
        for s in segments:
            _, _, off, rg = spans[s]
            cov[rows_at(s, core, me, 1)] = mine[off : off + rg] * (1.0 / total)
            for d in range(1, 8):
                go(close_by(s, d, me))

    def far(segments):
        for s in segments:
            for d in range(1, 8):
                from_there = (u * 4 + lax.rem(v + 4 - d // 2, 4)) * 2 + lax.rem(xh + d, 2)
                close_by(s, d, from_there).wait_recv()
            for d in range(1, 4):
                go(over_u(s, d, u))
            go(to_twin(s, 0, core, u))

    def relay(s):
        for d in range(1, 4):
            pu = lax.rem(u + 4 - d, 4)
            over_u(s, d, pu).wait_recv()
            go(to_twin(s, d, core, pu))

    def ready(s):
        twin_u = y + core * (z - y)
        for d in range(4):
            to_twin(s, d, 1 - core, lax.rem(twin_u + 4 - d, 4)).wait_recv()

    rows = lax.broadcasted_iota(jnp.int32, (B, B), 0)
    lanes = lax.broadcasted_iota(jnp.int32, (B, B), 1)
    bad[...] = jnp.zeros_like(bad)
    early, late = range(EARLY), range(EARLY, len(spans))
    reduce(0)
    near(early)
    far(early)
    reduce(1)
    near(late)
    relay(0)
    far(late)
    needs = {0: 0, 1: 1, 2: 2, 3: 3, 5: 4}

    def remainder(i, k):
        first = (starts[k] - k + i) * B
        value = cov[pl.ds(first if isinstance(i, int) else pl.multiple_of(first, B), B)]
        if k:
            ib = pl.ds(i * B if isinstance(i, int) else pl.multiple_of(i * B, B), B)
            kb, done = slice(k * B, (k + 1) * B), slice(0, k * B)
            value = value - dot3((lh[ib, done], ll[ib, done]), (lh[kb, done], ll[kb, done]), NT)
        return value

    def panel(i, k):
        ib, kb = slice(i * B, (i + 1) * B), slice(k * B, (k + 1) * B)
        lh[ib, kb], ll[ib, kb] = halves(dot3(halves(g[i]), (lh[kb, kb], ll[kb, kb]), NT))

    def pivot(k):
        kb = slice(k * B, (k + 1) * B)
        inverse_factor(g.at[k], m_scr, bad)
        lh[kb, kb], ll[kb, kb] = halves(m_scr[...])

    def whiten(k):
        kb, done = slice(k * B, (k + 1) * B), slice(0, k * B)
        f = feat[core, k].astype(jnp.float32)
        if k:
            f = f - dot3((wh[:, done], wl[:, done]), (lh[kb, done], ll[kb, done]), NT)
        whi, wlo = halves(dot3(halves(f), (lh[kb, kb], ll[kb, kb]), NT))
        w_send[k] = whi
        if k < nb - 1:
            wh[:, kb], wl[:, kb] = whi, wlo

    ready(0)
    diagonal = jnp.where(rows == lanes, ridge, 0.0)
    g[0] = remainder(0, 0) + diagonal
    for i in range(1, nb):
        g[i] = remainder(i, 0)
    pivot(0)
    for k in range(nb):
        if k < nb - 1:
            panel(k + 1, k)
        if k + 1 < len(spans):
            relay(k + 1)
        if k < nb - 1:
            if k + 1 in needs:
                ready(needs[k + 1])
            g[k + 1] = remainder(k + 1, k + 1) + diagonal
            pivot(k + 1)
            for i in range(k + 2, nb):
                panel(i, k)
        for i in range(k + 2, nb):
            g[i] = remainder(i, k + 1)
        whiten(k)
        go(push(w_send.at[k], w_recv.at[k], w_s.at[k], w_r.at[k], blk=1 - view))
    flags = push(bad, bad2, w_s.at[nb], w_r.at[nb], blk=1 - view)
    flags.start()

    half = text_ref.shape[0]
    own = pl.ds(pl.multiple_of(view * half, half), half)
    away = pl.ds(pl.multiple_of((1 - view) * half, half), half)
    for k in reversed(range(nb)):
        push(w_send.at[k], w_recv.at[k], w_s.at[k], w_r.at[k], blk=1 - view).wait_recv()
    for k in reversed(range(nb)):
        kb = slice(k * B, (k + 1) * B)
        rest = w_recv[k].astype(jnp.float32) if k == nb - 1 else g[k]
        value = dot3(halves(rest), (lh[kb, kb], ll[kb, kb]), NN)
        num[...] = value
        back[k] = num[away].astype(jnp.bfloat16)
        go(push(back.at[k], returned.at[k], b_s.at[k], b_r.at[k], blk=1 - view))
        text_ref[:, kb] = num[own]
        quant_ref[:, kb] = num[own]
        found = halves(value)
        for j in reversed(range(k)):
            jb = slice(j * B, (j + 1) * B)
            rest = w_recv[j].astype(jnp.float32) if k == nb - 1 else g[j]
            g[j] = rest - dot3(found, (lh[kb, jb], ll[kb, jb]), NN)
    for k in reversed(range(nb)):
        kb = slice(k * B, (k + 1) * B)
        push(back.at[k], returned.at[k], b_s.at[k], b_r.at[k], blk=1 - view).wait_recv()
        theirs = returned[k].astype(jnp.float32)

        @pl.when(view == 0)
        def _():
            quant_ref[:, kb] = theirs

        @pl.when(view == 1)
        def _():
            text_ref[:, kb] = theirs

    flags.wait()
    flag_ref[0] = jnp.sum(bad[...] + bad2[...])
    for copy in sent:
        copy.wait_send()
    for w in range(2):
        lax.fori_loop(1, peers, lambda d, _: (scatter(w, d).wait_send(), 0)[1], 0)


def whole_step(text_emb, quant_emb, text_head, quant_head, peers, total):
    rows, emb = text_emb.shape
    n = 2 * text_head.shape[1]
    assert emb == 2 * n
    nb = n // B
    blocks = nb * (nb + 1) // 4
    chunk = blocks * B // peers
    segs = len(SEGMENTS)
    dma = pltpu.SemaphoreType.DMA
    bf = jnp.bfloat16
    f32 = jnp.float32
    return pl.pallas_call(
        functools.partial(step_kernel, total, ridge_weight),
        out_shape=[jax.ShapeDtypeStruct((rows // 2, n), f32)] * 2 + [jax.ShapeDtypeStruct((1,), f32)],
        in_specs=[HBM] * 4,
        out_specs=[VMEM] * 2 + [pl.BlockSpec(memory_space=pltpu.SMEM)],
        scratch_shapes=[
            pltpu.VMEM((2, nb, rows, B), bf),
            pltpu.VMEM((nb // 2, rows, B), bf),
            pltpu.VMEM((peers, chunk, B), bf),
            pltpu.VMEM((peers, chunk, B), bf),
            pltpu.VMEM((chunk, B), f32),
            pltpu.VMEM((2 * blocks * B, B), f32),
            pltpu.VMEM((n, n), bf),
            pltpu.VMEM((n, n), bf),
            pltpu.VMEM((nb, B, B), f32),
            pltpu.VMEM((B, B), f32),
            pltpu.VMEM((rows, n), bf),
            pltpu.VMEM((rows, n), bf),
            pltpu.VMEM((nb, rows, B), bf),
            pltpu.VMEM((nb, rows, B), bf),
            pltpu.VMEM((rows, n), bf),
            pltpu.VMEM((rows, n), bf),
            pltpu.VMEM((rows, B), f32),
            pltpu.VMEM((nb, rows // 2, B), bf),
            pltpu.VMEM((nb, rows // 2, B), bf),
            pltpu.VMEM((8, B), f32),
            pltpu.VMEM((8, B), f32),
            dma((2, nb + 2)),
            dma((3, nb // 2)),
            dma((3, nb // 2)),
            dma((2, peers)),
            dma((2, peers)),
            dma((segs, 8)),
            dma((segs, 8)),
            dma((segs, 4)),
            dma((segs, 4)),
            dma((segs, 4)),
            dma((segs, 4)),
            dma((nb + 1,)),
            dma((nb + 1,)),
            dma((nb,)),
            dma((nb,)),
        ],
        compiler_params=pltpu.CompilerParams(collective_id=0, has_side_effects=True, vmem_limit_bytes=60 << 20),
    )(text_emb, quant_emb, text_head, quant_head)


def direct_kernel(c_ref, m_ref, panel):
    nb = c_ref.shape[0] // B
    rows = lax.broadcasted_iota(jnp.int32, (B, B), 0)
    cols = lax.broadcasted_iota(jnp.int32, (B, B), 1)
    lane = lax.broadcasted_iota(jnp.int32, (1, B), 1)
    sub = lax.broadcasted_iota(jnp.int32, (B, 1), 0)

    def exact(a, b, dims):
        return lax.dot_general(a, b, dims, precision=lax.Precision.HIGHEST, preferred_element_type=jnp.float32)

    def at(i):
        return pl.ds(pl.multiple_of(i * B, B), B)

    def init(i, _):
        def column(j, _):
            m_ref[at(i), at(j)] = jnp.where(j > i, 0.0, c_ref[at(i), at(j)])
            return 0

        return lax.fori_loop(0, nb, column, 0)

    lax.fori_loop(0, nb, init, 0)

    def step(k, _):
        kb = at(k)
        panel[k] = m_ref[kb, kb]

        def pivot(j, _):
            s = panel[k]
            row = panel[k, pl.ds(j, 1), :]
            p = jnp.sum(jnp.where(lane == j, row, 0.0), axis=1, keepdims=True)
            col = jnp.sum(jnp.where(cols == j, s, 0.0), axis=1, keepdims=True)
            below = sub > j
            pivot_row = jnp.where(lane == j, 1.0, row)
            left = jnp.where(jnp.logical_and(cols == j, below), 0.0, s)
            panel[k] = left - jnp.where(below, col / p, 0.0) * pivot_row
            panel[k, pl.ds(j, 1), :] = jnp.where(lane <= j, pivot_row, 0.0) * lax.rsqrt(p)
            return 0

        lax.fori_loop(0, B, pivot, 0)
        m_ref[kb, kb] = panel[k]

        def inverse_row(j, _):
            m_ref[kb, at(j)] = exact(m_ref[kb, kb], m_ref[kb, at(j)], NN)
            return 0

        lax.fori_loop(0, k, inverse_row, 0)

        def factor(i, _):
            panel[i] = exact(m_ref[at(i), kb], m_ref[kb, kb], NT)
            m_ref[at(i), kb] = jnp.zeros((B, B), jnp.float32)
            return 0

        lax.fori_loop(k + 1, nb, factor, 0)

        def update(i, _):
            def inverse_part(j, _):
                m_ref[at(i), at(j)] = m_ref[at(i), at(j)] - exact(panel[i], m_ref[kb, at(j)], NN)
                return 0

            lax.fori_loop(0, k + 1, inverse_part, 0)

            def schur(j, _):
                m_ref[at(i), at(j)] = m_ref[at(i), at(j)] - exact(panel[i], panel[j], NT)
                return 0

            return lax.fori_loop(k + 1, i + 1, schur, 0)

        return lax.fori_loop(k + 1, nb, update, 0)

    lax.fori_loop(0, nb, step, 0)


def direct_step(text_emb, quant_emb, text_head, quant_head, total):
    view = lax.axis_index("blk")
    ranks = lax.axis_size("rows")
    h = jnp.stack(
        [
            jnp.dot(text_emb, text_head, preferred_element_type=jnp.float32).astype(jnp.bfloat16),
            jnp.dot(quant_emb, quant_head, preferred_element_type=jnp.float32).astype(jnp.bfloat16),
        ]
    )

    def swapped(x):
        return lax.ppermute(x, "blk", [(0, 1), (1, 0)])

    near = lax.dynamic_index_in_dim(h, view, 0, keepdims=False)
    far = swapped(lax.dynamic_index_in_dim(h, 1 - view, 0, keepdims=False))
    feat = jnp.where(view == 0, jnp.concatenate([near, far], 1), jnp.concatenate([far, near], 1))
    n = feat.shape[1]
    cov = mm(feat, feat, TN)
    hop = 1
    while hop < ranks:
        cov = cov + lax.ppermute(cov, "rows", [(r, r ^ hop) for r in range(ranks)])
        hop *= 2
    cov = cov / total + ridge_weight * jnp.eye(n, dtype=jnp.float32)
    inverse = pl.pallas_call(
        direct_kernel,
        out_shape=jax.ShapeDtypeStruct((n, n), jnp.float32),
        in_specs=[VMEM],
        out_specs=VMEM,
        scratch_shapes=[pltpu.VMEM((n // B, B, B), jnp.float32)],
        compiler_params=pltpu.CompilerParams(vmem_limit_bytes=56 << 20),
    )(cov)
    exact = functools.partial(
        lax.dot_general, precision=lax.Precision.HIGHEST, preferred_element_type=jnp.float32
    )
    white = swapped(exact(feat.astype(jnp.float32), inverse, NT))
    grad = exact(white, inverse, NN)
    half = grad.shape[0] // 2
    own = lax.dynamic_slice_in_dim(grad, view * half, half, 0)
    other = swapped(lax.dynamic_slice_in_dim(grad, (1 - view) * half, half, 0))
    return jnp.where(view == 0, own, other), jnp.where(view == 0, other, own)


def shards(*arrays):
    peers = lax.axis_size("rows") // 2
    total = arrays[0].shape[0] * lax.axis_size("rows")
    text, quant, flag = whole_step(*arrays, peers, total)
    return lax.cond(flag[0] > 0, lambda: direct_step(*arrays, total), lambda: (text + flag[0], quant + flag[0]))


def solution(mesh):
    placed = (P("rows", None), P("rows", None), P(None, "blk"), P(None, "blk"))
    return jax.shard_map(
        shards,
        mesh=mesh,
        in_specs=placed,
        out_specs=(P(("rows", "blk"), None), P(("rows", "blk"), None)),
        check_vma=False,
    )
```

```python
import functools

import jax
import jax.numpy as jnp
from jax import lax
from jax.experimental import pallas as pl
from jax.experimental.pallas import tpu as pltpu
from jax.sharding import PartitionSpec as P

ridge_weight = 0.05
B = 256
NN = (((1,), (0,)), ((), ()))
NT = (((1,), (1,)), ((), ()))
TN = (((0,), (0,)), ((), ()))
MESH = pl.DeviceIdType.MESH
VMEM = pl.BlockSpec(memory_space=pltpu.VMEM)
HBM = pl.BlockSpec(memory_space=pl.ANY)


def mm(a, b, dims):
    return lax.dot_general(a, b, dims, preferred_element_type=jnp.float32)


def halves(x):
    hi = x.astype(jnp.bfloat16)
    return hi, (x - hi.astype(jnp.float32)).astype(jnp.bfloat16)


def dot3(a, b, dims):
    (ah, al), (bh, bl) = a, b
    return mm(ah, bh, dims) + (mm(ah, bl, dims) + mm(al, bh, dims))


def push(src, dst, send, recv, **device):
    return pltpu.make_async_remote_copy(
        src_ref=src, dst_ref=dst, send_sem=send, recv_sem=recv, device_id=device, device_id_type=MESH
    )

SEGMENTS = ((0, 4), (8, 4), (16, 4), (24, 4), (32, 2))
EARLY = 3


def inverse_factor(s_ref, m_ref, bad_ref):
    rows = lax.broadcasted_iota(jnp.int32, (B, B), 0)
    cols = lax.broadcasted_iota(jnp.int32, (B, B), 1)
    eye = jnp.where(rows == cols, 1.0, 0.0)
    weight = jnp.where(rows > cols, 1.0, jnp.where(rows == cols, 0.5, 0.0))
    s = s_ref[...]
    on = jnp.where(rows == cols, s, 0.0)
    sc = lax.rsqrt(jnp.sum(on, axis=1, keepdims=True))
    sr = lax.rsqrt(jnp.sum(on, axis=0, keepdims=True))
    a = jnp.where(rows == cols, 1.0, s * sc * sr)
    step = eye - weight * (a - eye)
    m_ref[...] = step * sr
    bf = jnp.bfloat16
    t = (eye - weight * (a - eye)).astype(bf)
    a = mm(mm(t, a.astype(bf), NN).astype(bf), t, NT)
    t = (eye - weight * (a - eye)).astype(bf)
    m_ref[...] = mm(t, m_ref[...].astype(bf), NN)
    a = mm(mm(t, a.astype(bf), NN).astype(bf), t, NT)
    t = (eye - weight * (a - eye)).astype(bf)
    m_ref[...] = mm(t, m_ref[...].astype(bf), NN)
    t = halves(m_ref[...])
    gap = dot3(halves(dot3(t, halves(s_ref[...]), NN)), t, NT) - eye
    far_off = jnp.sum(jnp.sum(gap * gap, axis=0, keepdims=True), axis=1, keepdims=True)
    bad_ref[...] += jnp.where(far_off <= 0.06, 0.0, 1.0)
    m_ref[...] = dot3(halves(eye - weight * gap), halves(m_ref[...]), NN)


def step_kernel(
    total, ridge, text_emb, quant_emb, text_head, quant_head, text_ref, quant_ref, flag_ref,
    feat, away_feat, part, arrived, mine, cov, lh, ll, g, m_scr, wh, wl, w_send, w_recv, gh, gl, num, back, returned, bad, bad2,
    h_sem, e_send, e_recv, s_send, s_recv, v_send, v_recv, u_send, u_recv, t_send, t_recv, w_s, w_r, b_s, b_r,
):
    at = lax.axis_index("rows")
    view = lax.axis_index("blk")
    core, xh, y, z = lax.rem(at, 2), lax.rem(at // 2, 2), lax.rem(at // 4, 4), at // 16
    twin = at + 1 - 2 * core
    peers = arrived.shape[0]
    nb = lh.shape[0] // B
    per = nb // 2
    starts = [sum(nb - c for c in range(k)) for k in range(nb)]
    order = [(i, j) for j in range(nb) for i in range(j, nb)]
    u, v = z + core * (y - z), y + core * (z - y)

    def device(p_u, p_v, p_x):
        pz, py = p_u + core * (p_v - p_u), p_v + core * (p_u - p_v)
        return ((pz * 4 + py) * 2 + p_x) * 2 + core

    def device_of(p):
        return device(p // 8, lax.rem(p // 2, 4), lax.rem(p, 2))

    me = (u * 4 + v) * 2 + xh

    depth = text_emb.shape[1] // 2
    places = ((wh, wl, lh), (gh, gl, ll))

    def for_view(which, text, quant):
        @pl.when(view == 1 - which)
        def _():
            text()

        @pl.when(view == which)
        def _():
            quant()

    def emb_copy(src, which, half):
        part_of = src.at[:, half * depth : (half + 1) * depth]
        return pltpu.make_async_copy(part_of, places[which][half], h_sem.at[which, 2 * per + half])

    def head_copy(src, which, half, c):
        part_of = src.at[half * depth : (half + 1) * depth, c * B : (c + 1) * B]
        at_cols = slice((half * per + c) * B, (half * per + c + 1) * B)
        return pltpu.make_async_copy(part_of, places[which][2].at[:, at_cols], h_sem.at[which, 2 * c + half])

    def fetch(turn):
        which, c = turn // per, turn % per

        def start(emb, head):
            for half in range(2):
                if c == 0:
                    emb_copy(emb, which, half).start()
                head_copy(head, which, half, c).start()

        for_view(which, lambda: start(text_emb, text_head), lambda: start(quant_emb, quant_head))

    for turn in range(2):
        fetch(turn)

    barrier = pltpu.get_barrier_semaphore()

    def greet(d, _):
        pl.semaphore_signal(barrier, inc=1, device_id={"rows": device_of(lax.rem(me + d, peers))}, device_id_type=MESH)
        return 0

    pl.semaphore_signal(barrier, inc=1, device_id={"blk": 1 - view}, device_id_type=MESH)
    pl.semaphore_signal(barrier, inc=1, device_id={"rows": twin}, device_id_type=MESH)
    lax.fori_loop(1, peers, greet, 0)

    def project(which, c):
        emb0, emb1, head = places[which]
        for half in range(2):
            head_copy(text_head, which, half, c).wait()
        lo, hi = slice(c * B, (c + 1) * B), slice((per + c) * B, (per + c + 1) * B)
        return (mm(emb0[...], head[:, lo], NN) + mm(emb1[...], head[:, hi], NN)).astype(jnp.bfloat16)

    sent = []

    def go(copy):
        copy.start()
        sent.append(copy)

    def swap(c, which_view):
        return push(away_feat.at[c], feat.at[core, which_view * per + c], e_send.at[0, c], e_recv.at[0, c], blk=1 - view)

    def share(turn, which_core, b):
        c = lax.rem(b, per)
        block = feat.at[which_core, b]
        return push(block, block, e_send.at[turn, c], e_recv.at[turn, c], rows=twin)

    for which in range(2):
        for half in range(2):
            emb_copy(text_emb, which, half).wait()
        for c in range(per):
            if which * per + c + 2 < 2 * per:
                fetch(which * per + c + 2)
            if which == 0:
                away_feat[c] = project(which, c)
                if c == 0:
                    pl.semaphore_wait(barrier, peers + 1)
                go(swap(c, view))
            else:
                feat[core, view * per + c] = project(which, c)
                go(share(1, core, view * per + c))
    for c in range(per):
        swap(c, 1 - view).wait_recv()
        go(share(2, core, (1 - view) * per + c))
    for c in range(per):
        share(1, 1 - core, view * per + c).wait_recv()
    for c in range(per):
        share(2, 1 - core, (1 - view) * per + c).wait_recv()

    offset = 0
    spans = []
    for begin, count in SEGMENTS:
        rg = count * B // peers
        spans.append((begin, count, offset, rg))
        offset += rg

    def products(segments):
        for begin, count, off, rg in segments:
            for t in range(count):
                (i0, j0), (i1, j1) = order[begin + t], order[begin + count + t]
                i, j = i0 + core * (i1 - i0), j0 + core * (j1 - j0)
                block = mm(feat[0, i], feat[0, j], TN) + mm(feat[1, i], feat[1, j], TN)
                n = B // rg
                part[t * n : (t + 1) * n, off : off + rg] = block.astype(jnp.bfloat16).reshape(n, rg, B)

    cut = spans[EARLY][2]
    waves = [(0, cut), (cut, mine.shape[0] - cut)]

    def scatter(w, d):
        p = lax.rem(me + d, peers)
        piece = pl.ds(*waves[w])
        return push(part.at[p, piece], arrived.at[me, piece], s_send.at[w, d], s_recv.at[w, d], rows=device_of(p))

    def landed(w, d):
        p = lax.rem(me + peers - d, peers)
        piece = pl.ds(*waves[w])
        return push(part.at[p, piece], arrived.at[p, piece], s_send.at[w, d], s_recv.at[w, d], rows=device_of(p))

    for w, segments in enumerate((spans[:EARLY], spans[EARLY:])):
        products(segments)
        lax.fori_loop(1, peers, lambda d, _: (scatter(w, d).start(), 0)[1], 0)

    def reduce(w):
        piece = pl.ds(*waves[w])
        mine[piece] = part[me, piece].astype(jnp.float32)

        def add(d, _):
            landed(w, d).wait_recv()
            mine[piece] += arrived[lax.rem(me + peers - d, peers), piece].astype(jnp.float32)
            return 0

        lax.fori_loop(1, peers, add, 0)

    def rows_at(s, c, piece, count):
        begin, size, _, rg = spans[s]
        return pl.ds(pl.multiple_of((begin + c * size) * B + piece * rg, 16), count * rg)

    def same(rows, send, recv, dev):
        return push(cov.at[rows], cov.at[rows], send, recv, rows=dev)

    def close_by(s, d, piece):
        there = device(u, lax.rem(v + d // 2, 4), lax.rem(xh + d, 2))
        return same(rows_at(s, core, piece, 1), v_send.at[s, d], v_recv.at[s, d], there)

    def over_u(s, d, pu):
        return same(rows_at(s, core, pu * 8, 8), u_send.at[s, d], u_recv.at[s, d], device(lax.rem(u + d, 4), v, xh))

    def to_twin(s, d, c, pu):
        return same(rows_at(s, c, pu * 8, 8), t_send.at[s, d], t_recv.at[s, d], twin)

    def near(segments):
        for s in segments:
            _, _, off, rg = spans[s]
            cov[rows_at(s, core, me, 1)] = mine[off : off + rg] * (1.0 / total)
            for d in range(1, 8):
                go(close_by(s, d, me))

    def far(segments):
        for s in segments:
            for d in range(1, 8):
                from_there = (u * 4 + lax.rem(v + 4 - d // 2, 4)) * 2 + lax.rem(xh + d, 2)
                close_by(s, d, from_there).wait_recv()
            for d in range(1, 4):
                go(over_u(s, d, u))
            go(to_twin(s, 0, core, u))

    def relay(s):
        for d in range(1, 4):
            pu = lax.rem(u + 4 - d, 4)
            over_u(s, d, pu).wait_recv()
            go(to_twin(s, d, core, pu))

    def ready(s):
        twin_u = y + core * (z - y)
        for d in range(4):
            to_twin(s, d, 1 - core, lax.rem(twin_u + 4 - d, 4)).wait_recv()

    rows = lax.broadcasted_iota(jnp.int32, (B, B), 0)
    lanes = lax.broadcasted_iota(jnp.int32, (B, B), 1)
    bad[...] = jnp.zeros_like(bad)
    early, late = range(EARLY), range(EARLY, len(spans))
    reduce(0)
    near(early)
    far(early)
    reduce(1)
    near(late)
    relay(0)
    far(late)
    needs = {0: 0, 1: 1, 2: 2, 3: 3, 5: 4}

    def remainder(i, k):
        first = (starts[k] - k + i) * B
        value = cov[pl.ds(first if isinstance(i, int) else pl.multiple_of(first, B), B)]
        if k:
            ib = pl.ds(i * B if isinstance(i, int) else pl.multiple_of(i * B, B), B)
            kb, done = slice(k * B, (k + 1) * B), slice(0, k * B)
            value = value - dot3((lh[ib, done], ll[ib, done]), (lh[kb, done], ll[kb, done]), NT)
        return value

    def panel(i, k):
        ib, kb = slice(i * B, (i + 1) * B), slice(k * B, (k + 1) * B)
        lh[ib, kb], ll[ib, kb] = halves(dot3(halves(g[i]), (lh[kb, kb], ll[kb, kb]), NT))

    def pivot(k):
        kb = slice(k * B, (k + 1) * B)
        inverse_factor(g.at[k], m_scr, bad)
        lh[kb, kb], ll[kb, kb] = halves(m_scr[...])

    def whiten(k):
        kb, done = slice(k * B, (k + 1) * B), slice(0, k * B)
        f = feat[core, k].astype(jnp.float32)
        if k:
            f = f - dot3((wh[:, done], wl[:, done]), (lh[kb, done], ll[kb, done]), NT)
        whi, wlo = halves(dot3(halves(f), (lh[kb, kb], ll[kb, kb]), NT))
        w_send[k] = whi
        if k < nb - 1:
            wh[:, kb], wl[:, kb] = whi, wlo

    ready(0)
    diagonal = jnp.where(rows == lanes, ridge, 0.0)
    g[0] = remainder(0, 0) + diagonal
    for i in range(1, nb):
        g[i] = remainder(i, 0)
    pivot(0)
    for k in range(nb):
        if k < nb - 1:
            panel(k + 1, k)
        if k + 1 < len(spans):
            relay(k + 1)
        if k < nb - 1:
            if k + 1 in needs:
                ready(needs[k + 1])
            g[k + 1] = remainder(k + 1, k + 1) + diagonal
            pivot(k + 1)
            for i in range(k + 2, nb):
                panel(i, k)
        for i in range(k + 2, nb):
            g[i] = remainder(i, k + 1)
        whiten(k)
        go(push(w_send.at[k], w_recv.at[k], w_s.at[k], w_r.at[k], blk=1 - view))
    flags = push(bad, bad2, w_s.at[nb], w_r.at[nb], blk=1 - view)
    flags.start()

    half = text_ref.shape[0]
    own = pl.ds(pl.multiple_of(view * half, half), half)
    away = pl.ds(pl.multiple_of((1 - view) * half, half), half)
    for k in reversed(range(nb)):
        push(w_send.at[k], w_recv.at[k], w_s.at[k], w_r.at[k], blk=1 - view).wait_recv()
    for k in reversed(range(nb)):
        kb = slice(k * B, (k + 1) * B)
        rest = w_recv[k].astype(jnp.float32) if k == nb - 1 else g[k]
        value = dot3(halves(rest), (lh[kb, kb], ll[kb, kb]), NN)
        num[...] = value
        back[k] = num[away].astype(jnp.bfloat16)
        go(push(back.at[k], returned.at[k], b_s.at[k], b_r.at[k], blk=1 - view))
        text_ref[:, kb] = num[own]
        quant_ref[:, kb] = num[own]
        found = halves(value)
        for j in reversed(range(k)):
            jb = slice(j * B, (j + 1) * B)
            rest = w_recv[j].astype(jnp.float32) if k == nb - 1 else g[j]
            g[j] = rest - dot3(found, (lh[kb, jb], ll[kb, jb]), NN)
    for k in reversed(range(nb)):
        kb = slice(k * B, (k + 1) * B)
        push(back.at[k], returned.at[k], b_s.at[k], b_r.at[k], blk=1 - view).wait_recv()
        theirs = returned[k].astype(jnp.float32)

        @pl.when(view == 0)
        def _():
            quant_ref[:, kb] = theirs

        @pl.when(view == 1)
        def _():
            text_ref[:, kb] = theirs

    flags.wait()
    flag_ref[0] = jnp.sum(bad[...] + bad2[...])
    for copy in sent:
        copy.wait_send()
    for w in range(2):
        lax.fori_loop(1, peers, lambda d, _: (scatter(w, d).wait_send(), 0)[1], 0)


def whole_step(text_emb, quant_emb, text_head, quant_head, peers, total):
    rows, emb = text_emb.shape
    n = 2 * text_head.shape[1]
    assert emb == 2 * n
    nb = n // B
    blocks = nb * (nb + 1) // 4
    chunk = blocks * B // peers
    segs = len(SEGMENTS)
    dma = pltpu.SemaphoreType.DMA
    bf = jnp.bfloat16
    f32 = jnp.float32
    return pl.pallas_call(
        functools.partial(step_kernel, total, ridge_weight),
        out_shape=[jax.ShapeDtypeStruct((rows // 2, n), f32)] * 2 + [jax.ShapeDtypeStruct((1,), f32)],
        in_specs=[HBM] * 4,
        out_specs=[VMEM] * 2 + [pl.BlockSpec(memory_space=pltpu.SMEM)],
        scratch_shapes=[
            pltpu.VMEM((2, nb, rows, B), bf),
            pltpu.VMEM((nb // 2, rows, B), bf),
            pltpu.VMEM((peers, chunk, B), bf),
            pltpu.VMEM((peers, chunk, B), bf),
            pltpu.VMEM((chunk, B), f32),
            pltpu.VMEM((2 * blocks * B, B), f32),
            pltpu.VMEM((n, n), bf),
            pltpu.VMEM((n, n), bf),
            pltpu.VMEM((nb, B, B), f32),
            pltpu.VMEM((B, B), f32),
            pltpu.VMEM((rows, n), bf),
            pltpu.VMEM((rows, n), bf),
            pltpu.VMEM((nb, rows, B), bf),
            pltpu.VMEM((nb, rows, B), bf),
            pltpu.VMEM((rows, n), bf),
            pltpu.VMEM((rows, n), bf),
            pltpu.VMEM((rows, B), f32),
            pltpu.VMEM((nb, rows // 2, B), bf),
            pltpu.VMEM((nb, rows // 2, B), bf),
            pltpu.VMEM((8, B), f32),
            pltpu.VMEM((8, B), f32),
            dma((2, nb + 2)),
            dma((3, nb // 2)),
            dma((3, nb // 2)),
            dma((2, peers)),
            dma((2, peers)),
            dma((segs, 8)),
            dma((segs, 8)),
            dma((segs, 4)),
            dma((segs, 4)),
            dma((segs, 4)),
            dma((segs, 4)),
            dma((nb + 1,)),
            dma((nb + 1,)),
            dma((nb,)),
            dma((nb,)),
        ],
        compiler_params=pltpu.CompilerParams(collective_id=0, has_side_effects=True, vmem_limit_bytes=60 << 20),
    )(text_emb, quant_emb, text_head, quant_head)


def direct_kernel(c_ref, m_ref, panel):
    nb = c_ref.shape[0] // B
    rows = lax.broadcasted_iota(jnp.int32, (B, B), 0)
    cols = lax.broadcasted_iota(jnp.int32, (B, B), 1)
    lane = lax.broadcasted_iota(jnp.int32, (1, B), 1)
    sub = lax.broadcasted_iota(jnp.int32, (B, 1), 0)

    def exact(a, b, dims):
        return lax.dot_general(a, b, dims, precision=lax.Precision.HIGHEST, preferred_element_type=jnp.float32)

    def at(i):
        return pl.ds(pl.multiple_of(i * B, B), B)

    def init(i, _):
        def column(j, _):
            m_ref[at(i), at(j)] = jnp.where(j > i, 0.0, c_ref[at(i), at(j)])
            return 0

        return lax.fori_loop(0, nb, column, 0)

    lax.fori_loop(0, nb, init, 0)

    def step(k, _):
        kb = at(k)
        panel[k] = m_ref[kb, kb]

        def pivot(j, _):
            s = panel[k]
            row = panel[k, pl.ds(j, 1), :]
            p = jnp.sum(jnp.where(lane == j, row, 0.0), axis=1, keepdims=True)
            col = jnp.sum(jnp.where(cols == j, s, 0.0), axis=1, keepdims=True)
            below = sub > j
            pivot_row = jnp.where(lane == j, 1.0, row)
            left = jnp.where(jnp.logical_and(cols == j, below), 0.0, s)
            panel[k] = left - jnp.where(below, col / p, 0.0) * pivot_row
            panel[k, pl.ds(j, 1), :] = jnp.where(lane <= j, pivot_row, 0.0) * lax.rsqrt(p)
            return 0

        lax.fori_loop(0, B, pivot, 0)
        m_ref[kb, kb] = panel[k]

        def inverse_row(j, _):
            m_ref[kb, at(j)] = exact(m_ref[kb, kb], m_ref[kb, at(j)], NN)
            return 0

        lax.fori_loop(0, k, inverse_row, 0)

        def factor(i, _):
            panel[i] = exact(m_ref[at(i), kb], m_ref[kb, kb], NT)
            m_ref[at(i), kb] = jnp.zeros((B, B), jnp.float32)
            return 0

        lax.fori_loop(k + 1, nb, factor, 0)

        def update(i, _):
            def inverse_part(j, _):
                m_ref[at(i), at(j)] = m_ref[at(i), at(j)] - exact(panel[i], m_ref[kb, at(j)], NN)
                return 0

            lax.fori_loop(0, k + 1, inverse_part, 0)

            def schur(j, _):
                m_ref[at(i), at(j)] = m_ref[at(i), at(j)] - exact(panel[i], panel[j], NT)
                return 0

            return lax.fori_loop(k + 1, i + 1, schur, 0)

        return lax.fori_loop(k + 1, nb, update, 0)

    lax.fori_loop(0, nb, step, 0)


def direct_step(text_emb, quant_emb, text_head, quant_head, total):
    view = lax.axis_index("blk")
    ranks = lax.axis_size("rows")
    h = jnp.stack(
        [
            jnp.dot(text_emb, text_head, preferred_element_type=jnp.float32).astype(jnp.bfloat16),
            jnp.dot(quant_emb, quant_head, preferred_element_type=jnp.float32).astype(jnp.bfloat16),
        ]
    )

    def swapped(x):
        return lax.ppermute(x, "blk", [(0, 1), (1, 0)])

    near = lax.dynamic_index_in_dim(h, view, 0, keepdims=False)
    far = swapped(lax.dynamic_index_in_dim(h, 1 - view, 0, keepdims=False))
    feat = jnp.where(view == 0, jnp.concatenate([near, far], 1), jnp.concatenate([far, near], 1))
    n = feat.shape[1]
    cov = mm(feat, feat, TN)
    hop = 1
    while hop < ranks:
        cov = cov + lax.ppermute(cov, "rows", [(r, r ^ hop) for r in range(ranks)])
        hop *= 2
    cov = cov / total + ridge_weight * jnp.eye(n, dtype=jnp.float32)
    inverse = pl.pallas_call(
        direct_kernel,
        out_shape=jax.ShapeDtypeStruct((n, n), jnp.float32),
        in_specs=[VMEM],
        out_specs=VMEM,
        scratch_shapes=[pltpu.VMEM((n // B, B, B), jnp.float32)],
        compiler_params=pltpu.CompilerParams(vmem_limit_bytes=56 << 20),
    )(cov)
    exact = functools.partial(
        lax.dot_general, precision=lax.Precision.HIGHEST, preferred_element_type=jnp.float32
    )
    white = swapped(exact(feat.astype(jnp.float32), inverse, NT))
    grad = exact(white, inverse, NN)
    half = grad.shape[0] // 2
    own = lax.dynamic_slice_in_dim(grad, view * half, half, 0)
    other = swapped(lax.dynamic_slice_in_dim(grad, (1 - view) * half, half, 0))
    return jnp.where(view == 0, own, other), jnp.where(view == 0, other, own)


def shards(*arrays):
    peers = lax.axis_size("rows") // 2
    total = arrays[0].shape[0] * lax.axis_size("rows")
    text, quant, flag = whole_step(*arrays, peers, total)
    return lax.cond(flag[0] > 0, lambda: direct_step(*arrays, total), lambda: (text + flag[0], quant + flag[0]))


def solution(mesh):
    placed = (P("rows", None), P("rows", None), P(None, "blk"), P(None, "blk"))
    return jax.shard_map(
        shards,
        mesh=mesh,
        in_specs=placed,
        out_specs=(P(("rows", "blk"), None), P(("rows", "blk"), None)),
        check_vma=False,
    )
```
